128 devices in a mesh: chan: 64 (over x, z_hi, y, core), tm: 2 (over z_lo).
Axes of the slice: x: 4, y: 4, z: 4 (z_hi: 2, z_lo: 2; z = z_hi * 2 + z_lo), core: 2. Of those that a mesh axis runs over, the one named last changes fastest.
Arguments:
- spectra: bfloat16 [2, 64, 10240, 2, 384], P('tm', 'chan'), as said below
- mask: int32 [2, 64, 10240], P('tm', 'chan'), may hold values from 0 to 1, as said below
Outputs:
- correlations: float32 [8, 10240, 3001], P('tm', 'chan')
The draws below stay inside these ranges and needn't reach their ends.
Inputs may be any that keep to these rules, and one draw needn't show every extreme that they name: `spectra`: spectra of the windows, of scales that vary over bins and over channels. `mask`: in every window, among the 160 channels of one block (channels b * 160 to (b + 1) * 160 - 1) at most 120 flags are 1.
All inputs are finite; a program needn't handle non-finite values.
Results may differ from the reference program's by a relative error of at most 0.004.
Values may be sent and summed in bfloat16 or wider, within the bound.
No kernel may reach another device: no remote copies, remote signals or barrier semaphores. Data moves between devices by JAX's collectives and lax.ppermute only.
A program may use at most 192 MiB of HBM per device.

```python
import math
import jax
import jax.numpy as jnp
from jax import lax

CH = 10240
F = 384
F0 = 12
NFFT = 6000
MAXLAG = 1500
SB = 4
STEPS = 2
SRC = 8
LAGS = 3001
CH_DEV = 160
CAP = 120
WINS = 64
HALVES = 2


def draw_spectra(key, part):
    keys = jax.random.split(key, 3)
    shape = (HALVES, WINS, CH, 2, F)
    base = jax.random.normal(keys[0], shape, jnp.float32)
    column = jnp.exp(jax.random.uniform(keys[1], (F,), jnp.float32, 0.0, math.log(10.0)))
    row_scale = jnp.exp(jax.random.uniform(keys[2], (HALVES, WINS, CH, 1, 1), jnp.float32, 0.0, math.log(10.0)))
    return (base * column * row_scale).astype(jnp.bfloat16)


def draw_mask(key, part):
    keys = jax.random.split(key, 7)
    blocks = CH // CH_DEV
    windows = HALVES * WINS
    lanes = jnp.arange(CH_DEV, dtype=jnp.int32)
    dead_order = jax.random.randint(keys[0], (blocks, CH_DEV), 0, 65536) * CH_DEV + lanes
    dead_rank = jnp.argsort(jnp.argsort(dead_order, axis=1), axis=1)
    dead_count = jax.random.randint(keys[1], (blocks, 1), 0, CH_DEV - CAP + 1)
    dead = (dead_rank >= CH_DEV - dead_count).astype(jnp.int32)
    scores = jax.random.randint(keys[2], (windows, blocks, CH_DEV), 0, 65536) * CH_DEV + lanes + dead[None] * (65536 * CH_DEV)
    ranks = jnp.argsort(jnp.argsort(scores, axis=2), axis=2)
    floor_low = jax.random.randint(keys[3], (1, blocks), 1, CAP + 1)
    kept_count = jax.random.randint(keys[4], (windows, blocks), floor_low, CAP + 1)
    busiest = jax.random.randint(keys[5], (windows, 1), 0, blocks)
    fullest = jax.random.randint(keys[6], (1, 1), 0, blocks)
    block_index = jnp.arange(blocks, dtype=jnp.int32)[None, :]
    kept_count = jnp.where((block_index == busiest) | (block_index == fullest), CAP, kept_count)
    flags = (ranks < kept_count[..., None]).astype(jnp.int32)
    return flags.reshape(HALVES, WINS, CH)


def setup_inputs(seed: int = 0) -> dict:
    key_of = jax.random.split(jax.random.key(seed), 3)
    spectra = draw_spectra(jax.random.fold_in(key_of[2], 71), 0)
    mask = draw_mask(jax.random.fold_in(key_of[2], 71), 0)
    return {"spectra": spectra, "mask": mask}


def lag_table():
    bin_index = F0 + jnp.arange(F, dtype=jnp.int32)
    lag_index = jnp.arange(LAGS, dtype=jnp.int32) - MAXLAG
    phase_steps = jnp.mod(bin_index[:, None] * lag_index[None, :], NFFT)
    angles = phase_steps.astype(jnp.float32) * jnp.float32(2.0 * math.pi / NFFT)
    return jnp.concatenate([jnp.cos(angles), -jnp.sin(angles)], axis=0)

def whiten(window_spec, kept_mask):
    values = window_spec.astype(jnp.float32)
    energy = lax.optimization_barrier(jnp.sum(values * values, axis=(-2, -1))) / F
    factor = lax.rsqrt(energy + 1e-06) * kept_mask.astype(jnp.float32)
    return (values * factor[..., None, None]).astype(jnp.bfloat16)

def source_channels():
    which = jnp.arange(SRC, dtype=jnp.int32)
    return which // SB * (CH // CH_DEV // STEPS) * CH_DEV + which % SB

def reference(spectra, mask):
    chosen = source_channels()
    flat_spec = spectra.reshape(HALVES * WINS, CH, 2, F)
    flat_mask = mask.reshape(HALVES * WINS, CH)

    def add_window(totals, window):
        cross_sum, pair_count = totals
        window_spec, kept_mask = window
        whitened = whiten(window_spec, kept_mask).astype(jnp.float32)
        source_rows = whitened[chosen]
        source_keep = kept_mask[chosen].astype(jnp.float32)
        real_part = source_rows[:, None, 0] * whitened[None, :, 0] + source_rows[:, None, 1] * whitened[None, :, 1]
        imag_part = source_rows[:, None, 1] * whitened[None, :, 0] - source_rows[:, None, 0] * whitened[None, :, 1]
        cross_sum = cross_sum + jnp.stack([real_part, imag_part], axis=2)
        pair_count = pair_count + source_keep[:, None] * kept_mask.astype(jnp.float32)[None, :]
        return ((cross_sum, pair_count), None)
    start = (jnp.zeros((SRC, CH, 2, F), jnp.float32), jnp.zeros((SRC, CH), jnp.float32))
    (cross_sum, pair_count), _ = lax.scan(add_window, start, (flat_spec, flat_mask))
    lag_matrix = lag_table()

    def invert(pair_data):
        spectrum, counted = pair_data
        lagged = jnp.dot(spectrum.reshape(CH, 2 * F), lag_matrix, precision=lax.Precision.HIGHEST, preferred_element_type=jnp.float32)
        return lagged / jnp.maximum(counted, 1.0)[:, None]
    return lax.map(invert, (cross_sum, pair_count))
```

```python
import functools
import math

import jax
import jax.numpy as jnp
from jax import lax
from jax.experimental import pallas as pl
from jax.experimental.pallas import tpu as pltpu
from jax.sharding import PartitionSpec as P

CH = 10240
F = 384
F0 = 12
NFFT = 6000
MAXLAG = 1500
SB = 4
SRC = 8
LAGS = 3001
BLOCKS = 64
WIDE = 160
WINS = 64
SLOTS = 128
ROWS = 2 * SLOTS
BINS_A = 256
BINS_B = 128
STEP = 8
LAG_TILE = 512


def iota(shape, dim):
    return lax.broadcasted_iota(jnp.int32, shape, dim)


def one_hot(where):
    return jnp.where(where, 1.0, 0.0).astype(jnp.bfloat16)


def dot(a, b):
    return jnp.dot(a, b, preferred_element_type=jnp.float32)


def pack_kernel(tm_ref, mask_ref, x0, x1, x2, a0, a1, a2, b0, b1, b2, send_a, send_b, slot_ref, key_ref, src_ref, srcflag_ref):
    block = pl.program_id(0)

    @pl.when(block == 0)
    def _():
        flags = mask_ref[...].astype(jnp.float32).astype(jnp.bfloat16)
        lane = iota((WIDE, 2 * WIDE), 1)
        row = iota((WIDE, 2 * WIDE), 0)
        before = dot(flags, one_hot(row < lane // 2)).astype(jnp.int32)
        kept = dot(flags, one_hot(row == lane // 2))
        part = iota((BLOCKS, 2 * WIDE), 1) % 2
        slot_ref[...] = jnp.where(kept > 0.5, before + part * SLOTS, -1)
        lane = iota((WIDE, BINS_A), 1)
        row = iota((WIDE, BINS_A), 0)
        before = dot(flags, one_hot(row < lane))
        key_ref[...] = jnp.where(dot(flags, one_hot(row == lane)) > 0.5, before, -1.0)
        shift = SB * (1 - tm_ref[0])
        source = (lane + shift) % SRC
        first = dot(flags, one_hot((row == source % SB) & (source < SB) & (lane < SRC)))
        second = dot(flags, one_hot((row == source % SB) & (source >= SB) & (lane < SRC)))
        middle = BLOCKS // 2
        srcflag_ref[...] = first[0:1] + second[middle : middle + 1]
        take = iota((2 * SRC, 16), 0)
        lane = iota((2 * SRC, 16), 1)
        source = (take % SRC + shift) % SRC
        hit = lane == 2 * (source % SB) + take // SRC
        pick_a = one_hot(hit & (source < SB) & (kept[0:1, :16] > 0.5))
        pick_b = one_hot(hit & (source >= SB) & (kept[middle : middle + 1, :16] > 0.5))
        rows = [
            dot(pick_a, ra.reshape(16, 128)[...]) + dot(pick_b, rb.reshape(16, 128)[...])
            for ra, rb in ((a0, b0), (a1, b1), (a2, b2))
        ]
        squares = sum(r * r for r in rows)
        energy = jnp.sum(squares[:SRC] + squares[SRC:], axis=1, keepdims=True) / F
        factor = lax.rsqrt(energy + 1e-06)
        for k, r in enumerate(rows):
            src_ref[:SRC, k * 128 : (k + 1) * 128] = r[:SRC] * factor
            src_ref[SRC:, k * 128 : (k + 1) * 128] = r[SRC:] * factor

    slot = slot_ref[pl.ds(block, 1), :]
    pick = one_hot(iota((ROWS, 2 * WIDE), 0) == slot)
    band = jnp.concatenate([r.reshape(2 * WIDE, 128)[...] for r in (x0, x1, x2)], axis=1)
    rows = dot(pick, band)
    real, imag = rows[:SLOTS], rows[SLOTS:]
    energy = jnp.sum(real * real + imag * imag, axis=1, keepdims=True) / F
    factor = lax.rsqrt(energy + 1e-06)
    real = (real * factor).astype(jnp.bfloat16)
    imag = (imag * factor).astype(jnp.bfloat16)
    src = src_ref[...].astype(jnp.bfloat16)
    for out, lo, hi in ((send_a, 0, BINS_A), (send_b, BINS_A, F)):
        out[0, :SLOTS] = real[:, lo:hi]
        out[0, SLOTS:ROWS] = imag[:, lo:hi]
        out[0, SLOTS - SRC : SLOTS] = src[:SRC, lo:hi]
        out[0, ROWS - SRC : ROWS] = src[SRC:, lo:hi]
    line = iota((8, BINS_A), 0)
    notes = jnp.where(line == 0, key_ref[pl.ds(block, 1), :], jnp.where(line == 1, srcflag_ref[...], 0.0))
    send_a[0, ROWS : ROWS + 8] = notes.astype(jnp.bfloat16)


def pack(tm_index, mask, spectra):
    whole = lambda k: pl.BlockSpec((WIDE, 2, 128), lambda b: (b, 0, k))
    head = lambda k, at: pl.BlockSpec((8, 2, 128), lambda b: (at, 0, k))
    middle = BLOCKS // 2 * WIDE // 8
    return pl.pallas_call(
        pack_kernel,
        grid=(BLOCKS,),
        in_specs=[
            pl.BlockSpec(memory_space=pltpu.SMEM),
            pl.BlockSpec((BLOCKS, WIDE), lambda b: (0, 0)),
            *[whole(k) for k in range(3)],
            *[head(k, 0) for k in range(3)],
            *[head(k, middle) for k in range(3)],
        ],
        out_specs=[
            pl.BlockSpec((1, ROWS + 8, BINS_A), lambda b: (b, 0, 0)),
            pl.BlockSpec((1, ROWS, BINS_B), lambda b: (b, 0, 0)),
        ],
        out_shape=[
            jax.ShapeDtypeStruct((BLOCKS, ROWS + 8, BINS_A), jnp.bfloat16),
            jax.ShapeDtypeStruct((BLOCKS, ROWS, BINS_B), jnp.bfloat16),
        ],
        scratch_shapes=[
            pltpu.VMEM((BLOCKS, 2 * WIDE), jnp.int32),
            pltpu.VMEM((BLOCKS, BINS_A), jnp.float32),
            pltpu.VMEM((2 * SRC, F), jnp.float32),
            pltpu.VMEM((1, BINS_A), jnp.float32),
        ],
        cost_estimate=pl.CostEstimate(flops=2 * BLOCKS * ROWS * 2 * WIDE * F, bytes_accessed=30_000_000, transcendentals=0),
        compiler_params=pltpu.CompilerParams(vmem_limit_bytes=32 << 20),
        name="whiten_pack",
    )(tm_index, mask, *[spectra] * 9)


def spread_slots(got, pick, held, src, win, bins):
    held[win, :, :bins] = dot(pick, got[win, :SLOTS, :])
    held[win, :, bins:] = dot(pick, got[win, SLOTS:ROWS, :])
    src[win, :SRC] = got[win, SLOTS - SRC : SLOTS, :].astype(jnp.float32)
    src[win, SRC:] = got[win, ROWS - SRC : ROWS, :].astype(jnp.float32)


def correlate(held, src, outs, bins):
    def group(i, _):
        rows = pl.ds(pl.multiple_of(i * 8, 8), 8)
        for t in range(0, bins, 128):
            re_at, im_at = slice(t, t + 128), slice(bins + t, bins + t + 128)
            sums = [[ref[q, rows, re_at], ref[q, rows, im_at]] for ref, _ in outs for q in range(SB)]
            for win in range(STEP):
                b0, b1 = held[win, rows, re_at], held[win, rows, im_at]
                for n, q in enumerate([first + k for _, first in outs for k in range(SB)]):
                    a0 = jnp.broadcast_to(src[win, q : q + 1, re_at], (8, 128))
                    a1 = jnp.broadcast_to(src[win, SRC + q : SRC + q + 1, re_at], (8, 128))
                    sums[n][0] += a0 * b0 + a1 * b1
                    sums[n][1] += a1 * b0 - a0 * b1
            n = 0
            for ref, _ in outs:
                for q in range(SB):
                    ref[q, rows, re_at], ref[q, rows, im_at] = sums[n]
                    n += 1
        return 0

    lax.fori_loop(0, WIDE // 8, group, 0)


def first_kernel(got, theirs, mine, picks, count, held, src):
    @pl.when(pl.program_id(0) == 0)
    def _():
        theirs[...] = jnp.zeros_like(theirs)
        mine[...] = jnp.zeros_like(mine)
        count[...] = jnp.zeros_like(count)

    for win in range(STEP):
        notes = got[win, ROWS : ROWS + 8, :].astype(jnp.float32)
        key = jnp.transpose(notes)[:WIDE, 0:1]
        pick = one_hot(iota((WIDE, SLOTS), 1) == key.astype(jnp.int32))
        picks[win] = pick
        count[...] += jnp.where(key > -0.5, 1.0, 0.0) * notes[1:2, :128]
        spread_slots(got, pick, held, src, win, BINS_A)
    correlate(held, src, ((theirs, 0), (mine, SB)), BINS_A)


def first_sums(got):
    sums = jax.ShapeDtypeStruct((SB, WIDE, 2 * BINS_A), jnp.float32)
    sums_spec = pl.BlockSpec(sums.shape, lambda g: (0, 0, 0))
    return pl.pallas_call(
        first_kernel,
        grid=(WINS // STEP,),
        in_specs=[pl.BlockSpec((STEP, ROWS + 8, BINS_A), lambda g: (g, 0, 0))],
        out_specs=[
            sums_spec,
            sums_spec,
            pl.BlockSpec((STEP, WIDE, SLOTS), lambda g: (g, 0, 0)),
            pl.BlockSpec((WIDE, 128), lambda g: (0, 0)),
        ],
        out_shape=[
            sums,
            sums,
            jax.ShapeDtypeStruct((WINS, WIDE, SLOTS), jnp.bfloat16),
            jax.ShapeDtypeStruct((WIDE, 128), jnp.float32),
        ],
        scratch_shapes=[
            pltpu.VMEM((STEP, WIDE, 2 * BINS_A), jnp.float32),
            pltpu.VMEM((STEP, 2 * SRC, BINS_A), jnp.float32),
        ],
        cost_estimate=pl.CostEstimate(flops=30_000_000_000, bytes_accessed=20_000_000, transcendentals=0),
        compiler_params=pltpu.CompilerParams(vmem_limit_bytes=32 << 20),
        name="cross_sums_first",
    )(got)


def second_kernel(first, got, picks, out, held, src):
    @pl.when(pl.program_id(0) == 0)
    def _():
        out[...] = jnp.zeros_like(out)

    for win in range(STEP):
        spread_slots(got, picks[win], held, src, win, BINS_B)
    correlate(held, src, ((out, first),), BINS_B)


def second_sums(got, picks, first):
    sums = jax.ShapeDtypeStruct((SB, WIDE, 2 * BINS_B), jnp.float32)
    return pl.pallas_call(
        functools.partial(second_kernel, first),
        grid=(WINS // STEP,),
        in_specs=[
            pl.BlockSpec((STEP, ROWS, BINS_B), lambda g: (g, 0, 0)),
            pl.BlockSpec((STEP, WIDE, SLOTS), lambda g: (g, 0, 0)),
        ],
        out_specs=pl.BlockSpec(sums.shape, lambda g: (0, 0, 0)),
        out_shape=sums,
        scratch_shapes=[
            pltpu.VMEM((STEP, WIDE, 2 * BINS_B), jnp.float32),
            pltpu.VMEM((STEP, 2 * SRC, BINS_B), jnp.float32),
        ],
        cost_estimate=pl.CostEstimate(flops=8_000_000_000, bytes_accessed=8_000_000, transcendentals=0),
        compiler_params=pltpu.CompilerParams(vmem_limit_bytes=32 << 20),
        name="cross_sums_second",
    )(got, picks)


def split(x):
    high = x.astype(jnp.bfloat16)
    return high, (x - high.astype(jnp.float32)).astype(jnp.bfloat16)


def three_dots(high, low, table_high, table_low):
    t = table_high[...]
    return dot(high[...], t) + (dot(low[...], t) + dot(high[...], table_low[...]))


def load_sums(mine, theirs, high, low):
    total = mine[...] + theirs[...]
    h, rest = split(total)
    high[...] = h
    low[...] = rest


def lags_first_kernel(mine, theirs, table_high, table_low, out, high, low):
    @pl.when(pl.program_id(0) == 0)
    def _():
        load_sums(mine, theirs, high, low)

    out[...] = three_dots(high, low, table_high, table_low)


def lags_last_kernel(mine, theirs, table_high, table_low, before, count, count_theirs, out, high, low, scale):
    @pl.when(pl.program_id(0) == 0)
    def _():
        load_sums(mine, theirs, high, low)
        for q in range(SB):
            pairs = count[:, SB + q : SB + q + 1] + count_theirs[:, q : q + 1]
            scale[q * WIDE : (q + 1) * WIDE] = jnp.broadcast_to(1.0 / jnp.maximum(pairs, 1.0), (WIDE, 128))

    out[...] = (before[...] + three_dots(high, low, table_high, table_low)) * scale[:, 0:1]


def to_lags(mine, theirs, tables, before=None, counts=()):
    rows, depth = SB * WIDE, tables[0].shape[0]
    tile = pl.BlockSpec((rows, LAG_TILE), lambda n: (0, n))
    full = lambda shape: pl.BlockSpec(shape, lambda n: (0, 0))
    table = pl.BlockSpec((depth, LAG_TILE), lambda n: (0, n))
    last = before is not None
    return pl.pallas_call(
        lags_last_kernel if last else lags_first_kernel,
        grid=(pl.cdiv(LAGS, LAG_TILE),),
        in_specs=[full((rows, depth)), full((rows, depth)), table, table]
        + ([tile, full((WIDE, 128)), full((WIDE, 128))] if last else []),
        out_specs=tile,
        out_shape=jax.ShapeDtypeStruct((rows, LAGS), jnp.float32),
        scratch_shapes=[pltpu.VMEM((rows, depth), jnp.bfloat16)] * 2
        + ([pltpu.VMEM((rows, 128), jnp.float32)] if last else []),
        cost_estimate=pl.CostEstimate(flops=6 * rows * depth * LAGS, bytes_accessed=4 * rows * LAGS * (2 if last else 1), transcendentals=0),
        compiler_params=pltpu.CompilerParams(vmem_limit_bytes=32 << 20),
        name="to_lags_last" if last else "to_lags_first",
    )(
        mine.reshape(rows, depth),
        theirs.reshape(rows, depth),
        *tables,
        *((before, *counts) if last else ()),
    )


def lag_table(first_bin, bins, zero):
    bin_index = F0 + first_bin + zero + jnp.arange(bins, dtype=jnp.int32)
    lag_index = jnp.arange(LAGS, dtype=jnp.int32) - MAXLAG
    phase_steps = jnp.mod(bin_index[:, None] * lag_index[None, :], NFFT)
    angles = phase_steps.astype(jnp.float32) * jnp.float32(2.0 * math.pi / NFFT)
    table = jnp.concatenate([jnp.cos(angles), -jnp.sin(angles)], axis=0)
    high = lax.reduce_precision(table, 8, 7)
    return high.astype(jnp.bfloat16), (table - high).astype(jnp.bfloat16)


def swap(x):
    return lax.ppermute(x, "tm", [(0, 1), (1, 0)])


def local(spectra, mask):
    tm_index = lax.axis_index("tm").astype(jnp.int32)[None]
    send_a, send_b = pack(tm_index, mask.reshape(BLOCKS, WIDE), spectra.reshape(CH, 2, F))
    send_a, send_b, zero = lax.optimization_barrier((send_a, send_b, jnp.int32(0)))
    exchange = lambda x: lax.all_to_all(x, "chan", split_axis=0, concat_axis=0, tiled=True)
    got_a = exchange(send_a)
    got_b = exchange(send_b)
    tables_a = lag_table(0, BINS_A, zero)
    tables_b = lag_table(BINS_A, BINS_B, zero)
    theirs_a, mine_a, picks, count = first_sums(got_a)
    from_a = swap(theirs_a)
    count_from = swap(count)
    theirs_b = second_sums(got_b, picks, 0)
    from_b = swap(theirs_b)
    mine_b = second_sums(got_b, picks, SB)
    lagged = to_lags(mine_a, from_a, tables_a)
    lagged = to_lags(mine_b, from_b, tables_b, lagged, (count, count_from))
    return lagged.reshape(SB, WIDE, LAGS)


def solution(mesh):
    placed = (P("tm", "chan", None, None, None), P("tm", "chan", None))
    return jax.shard_map(
        local, mesh=mesh, in_specs=placed, out_specs=P("tm", "chan", None), check_vma=False
    )
```

```python
import functools
import math

import jax
import jax.numpy as jnp
from jax import lax
from jax.experimental import pallas as pl
from jax.experimental.pallas import tpu as pltpu
from jax.sharding import PartitionSpec as P

CH = 10240
F = 384
F0 = 12
NFFT = 6000
MAXLAG = 1500
SB = 4
SRC = 8
LAGS = 3001
BLOCKS = 64
WIDE = 160
WINS = 64
SLOTS = 128
ROWS = 2 * SLOTS
BINS_A = 256
BINS_B = 128
CAP = 120
PACK = 4
STEP_A = 16
STEP_B = 16
LAG_TILE = 512


def iota(shape, dim):
    return lax.broadcasted_iota(jnp.int32, shape, dim)


def one_hot(where):
    return jnp.where(where, 1.0, 0.0).astype(jnp.bfloat16)


def dot(a, b):
    return jnp.dot(a, b, preferred_element_type=jnp.float32)


def source_kernel(tm_ref, mask_ref, a0, a1, a2, b0, b1, b2, out):
    middle = BLOCKS // 2
    flags = mask_ref[...].astype(jnp.float32).astype(jnp.bfloat16)
    shift = SB * (1 - tm_ref[0])
    lane = iota((WIDE, 128), 1)
    row = iota((WIDE, 128), 0)
    source = (lane + shift) % SRC
    first = dot(flags, one_hot((row == source % SB) & (source < SB) & (lane < SRC)))
    second = dot(flags, one_hot((row == source % SB) & (source >= SB) & (lane < SRC)))
    kept = dot(flags, one_hot(row == lane // 2))
    take = iota((2 * SRC, 16), 0)
    lane = iota((2 * SRC, 16), 1)
    source = (take % SRC + shift) % SRC
    hit = lane == 2 * (source % SB) + take // SRC
    pick_a = one_hot(hit & (source < SB) & (kept[0:1, :16] > 0.5))
    pick_b = one_hot(hit & (source >= SB) & (kept[middle : middle + 1, :16] > 0.5))
    rows = [
        dot(pick_a, ra.reshape(16, 128)[...]) + dot(pick_b, rb.reshape(16, 128)[...])
        for ra, rb in ((a0, b0), (a1, b1), (a2, b2))
    ]
    squares = sum(r * r for r in rows)
    energy = jnp.sum(squares[:SRC] + squares[SRC:], axis=1, keepdims=True) / F
    factor = lax.rsqrt(energy + 1e-06)
    factor = jnp.concatenate([factor, factor], axis=0)
    for k, r in enumerate(rows):
        out[0, :, k * 128 : (k + 1) * 128] = (r * factor).astype(jnp.bfloat16)
    line = iota((2 * SRC, 128), 0)
    flag_line = first[0:1] + second[middle : middle + 1]
    out[0, :, F:] = jnp.where(line == 0, flag_line, 0.0).astype(jnp.bfloat16)


def source_rows(tm_index, mask, spectra):
    head = lambda k, at: pl.BlockSpec((8, 2, 128), lambda i: (at, 0, k))
    middle = BLOCKS // 2 * WIDE // 8
    return pl.pallas_call(
        source_kernel,
        grid=(1,),
        in_specs=[
            pl.BlockSpec(memory_space=pltpu.SMEM),
            pl.BlockSpec((BLOCKS, WIDE), lambda i: (0, 0)),
            *[head(k, 0) for k in range(3)],
            *[head(k, middle) for k in range(3)],
        ],
        out_specs=pl.BlockSpec((1, 2 * SRC, F + 128), lambda i: (0, 0, 0)),
        out_shape=jax.ShapeDtypeStruct((1, 2 * SRC, F + 128), jnp.bfloat16),
        cost_estimate=pl.CostEstimate(flops=10_000_000, bytes_accessed=100_000, transcendentals=0),
        name="source_rows",
    )(tm_index, mask, *[spectra] * 6)


def pack_kernel(mask_ref, x0, x1, x2, send_a, send_b, slot_ref, key_ref):
    step = pl.program_id(0)

    @pl.when(step == 0)
    def _():
        flags = mask_ref[...].astype(jnp.float32).astype(jnp.bfloat16)
        lane = iota((WIDE, 2 * WIDE), 1)
        row = iota((WIDE, 2 * WIDE), 0)
        before = dot(flags, one_hot(row < lane // 2))
        kept = dot(flags, one_hot(row == lane // 2))
        part = (iota((BLOCKS, 2 * WIDE), 1) % 2).astype(jnp.float32)
        slot_ref[...] = jnp.where(kept > 0.5, before + part * SLOTS, -1.0)
        lane = iota((WIDE, BINS_A), 1)
        row = iota((WIDE, BINS_A), 0)
        before = dot(flags, one_hot(row < lane))
        key_ref[...] = jnp.where(dot(flags, one_hot(row == lane)) > 0.5, before, -1.0)

    place = iota((ROWS, 2 * WIDE), 0).astype(jnp.float32).astype(jnp.bfloat16)
    for n in range(PACK):
        block = step * PACK + n
        slot = slot_ref[pl.ds(block, 1), :].astype(jnp.bfloat16)
        pick = jnp.where(place == slot, jnp.ones_like(place), jnp.zeros_like(place))
        at = pl.ds(n * 2 * WIDE, 2 * WIDE)
        band = jnp.concatenate([r.reshape(PACK * 2 * WIDE, 128)[at, :] for r in (x0, x1, x2)], axis=1)
        rows = dot(pick, band)
        real, imag = rows[:CAP], rows[SLOTS : SLOTS + CAP]
        energy = jnp.sum(real * real + imag * imag, axis=1, keepdims=True) / F
        factor = lax.rsqrt(energy + 1e-06)
        real = (real * factor).astype(jnp.bfloat16)
        imag = (imag * factor).astype(jnp.bfloat16)
        send_a[n, :CAP] = real[:, :BINS_A]
        send_a[n, CAP:SLOTS] = jnp.broadcast_to(key_ref[pl.ds(block, 1), :], (8, BINS_A)).astype(jnp.bfloat16)
        send_a[n, SLOTS:] = imag[:, :BINS_A]
        send_b[n, :CAP] = real[:, BINS_A:]
        send_b[n, CAP:] = imag[:, BINS_A:]


def pack(mask, spectra):
    band = lambda k: pl.BlockSpec((PACK * WIDE, 2, 128), lambda b: (b, 0, k))
    return pl.pallas_call(
        pack_kernel,
        grid=(BLOCKS // PACK,),
        in_specs=[pl.BlockSpec((BLOCKS, WIDE), lambda b: (0, 0)), *[band(k) for k in range(3)]],
        out_specs=[
            pl.BlockSpec((PACK, SLOTS + CAP, BINS_A), lambda b: (b, 0, 0)),
            pl.BlockSpec((PACK, 2 * CAP, BINS_B), lambda b: (b, 0, 0)),
        ],
        out_shape=[
            jax.ShapeDtypeStruct((BLOCKS, SLOTS + CAP, BINS_A), jnp.bfloat16),
            jax.ShapeDtypeStruct((BLOCKS, 2 * CAP, BINS_B), jnp.bfloat16),
        ],
        scratch_shapes=[
            pltpu.VMEM((BLOCKS, 2 * WIDE), jnp.float32),
            pltpu.VMEM((BLOCKS, BINS_A), jnp.float32),
        ],
        cost_estimate=pl.CostEstimate(flops=2 * BLOCKS * ROWS * 2 * WIDE * F, bytes_accessed=30_000_000, transcendentals=0),
        compiler_params=pltpu.CompilerParams(vmem_limit_bytes=56 << 20),
        name="whiten_pack",
    )(mask, *[spectra] * 3)


def spread_slots(real, imag, source, pick, held, src, win):
    held[win] = dot(pick, jnp.concatenate([real, imag], axis=1))
    src[win] = source.astype(jnp.float32)


def correlate(held, src, outs, bins, steps):
    def group(i, _):
        rows = pl.ds(pl.multiple_of(i * 8, 8), 8)
        for t in range(0, bins, 128):
            re_at, im_at = slice(t, t + 128), slice(bins + t, bins + t + 128)
            sums = [[ref[q, rows, re_at], ref[q, rows, im_at]] for ref, _ in outs for q in range(SB)]
            for win in range(steps):
                b0, b1 = held[win, rows, re_at], held[win, rows, im_at]
                for n, q in enumerate([first + k for _, first in outs for k in range(SB)]):
                    a0 = jnp.broadcast_to(src[win, q : q + 1, re_at], (8, 128))
                    a1 = jnp.broadcast_to(src[win, SRC + q : SRC + q + 1, re_at], (8, 128))
                    sums[n][0] += a0 * b0 + a1 * b1
                    sums[n][1] += a1 * b0 - a0 * b1
            n = 0
            for ref, _ in outs:
                for q in range(SB):
                    ref[q, rows, re_at], ref[q, rows, im_at] = sums[n]
                    n += 1
        return 0

    lax.fori_loop(0, WIDE // 8, group, 0)


def first_kernel(got, source, theirs, mine, picks, count, held, src, total):
    step = pl.program_id(0)

    @pl.when(step == 0)
    def _():
        total[...] = jnp.zeros_like(total)
        mine[...] = jnp.zeros_like(mine)
        count[...] = jnp.zeros_like(count)

    for win in range(STEP_A):
        notes = got[win, CAP:SLOTS, :].astype(jnp.float32)
        key = jnp.transpose(notes)[:WIDE, 0:1]
        pick = one_hot(iota((WIDE, SLOTS), 1) == key.astype(jnp.int32))
        picks[win] = pick
        flags = source[win, :, F:].astype(jnp.float32)[0:1]
        count[...] += jnp.where(key > -0.5, 1.0, 0.0) * flags
        spread_slots(got[win, :CAP, :], got[win, SLOTS:, :], source[win, :, :BINS_A], pick[:, :CAP], held, src, win)
    correlate(held, src, ((total, 0), (mine, SB)), BINS_A, STEP_A)

    @pl.when(step == pl.num_programs(0) - 1)
    def _():
        theirs[...] = total[...].astype(jnp.bfloat16)


def first_sums(got, source):
    shape = (SB, WIDE, 2 * BINS_A)
    sums_spec = pl.BlockSpec(shape, lambda g: (0, 0, 0))
    return pl.pallas_call(
        first_kernel,
        grid=(WINS // STEP_A,),
        in_specs=[
            pl.BlockSpec((STEP_A, SLOTS + CAP, BINS_A), lambda g: (g, 0, 0)),
            pl.BlockSpec((STEP_A, 2 * SRC, F + 128), lambda g: (g, 0, 0)),
        ],
        out_specs=[
            sums_spec,
            sums_spec,
            pl.BlockSpec((STEP_A, WIDE, SLOTS), lambda g: (g, 0, 0)),
            pl.BlockSpec((WIDE, 128), lambda g: (0, 0)),
        ],
        out_shape=[
            jax.ShapeDtypeStruct(shape, jnp.bfloat16),
            jax.ShapeDtypeStruct(shape, jnp.float32),
            jax.ShapeDtypeStruct((WINS, WIDE, SLOTS), jnp.bfloat16),
            jax.ShapeDtypeStruct((WIDE, 128), jnp.float32),
        ],
        scratch_shapes=[
            pltpu.VMEM((STEP_A, WIDE, 2 * BINS_A), jnp.float32),
            pltpu.VMEM((STEP_A, 2 * SRC, BINS_A), jnp.float32),
            pltpu.VMEM(shape, jnp.float32),
        ],
        cost_estimate=pl.CostEstimate(flops=30_000_000_000, bytes_accessed=20_000_000, transcendentals=0),
        compiler_params=pltpu.CompilerParams(vmem_limit_bytes=32 << 20),
        name="cross_sums_first",
    )(got, source)


def second_kernel(first, got, source, picks, out, held, src, total):
    step = pl.program_id(0)

    @pl.when(step == 0)
    def _():
        total[...] = jnp.zeros_like(total)

    for win in range(STEP_B):
        real, imag = got[win, :CAP, :], got[win, CAP:, :]
        spread_slots(real, imag, source[win], picks[win, :, :CAP], held, src, win)
    correlate(held, src, ((total, first),), BINS_B, STEP_B)

    @pl.when(step == pl.num_programs(0) - 1)
    def _():
        out[...] = total[...].astype(out.dtype)


def second_sums(got, source, picks, first, dtype):
    shape = (SB, WIDE, 2 * BINS_B)
    return pl.pallas_call(
        functools.partial(second_kernel, first),
        grid=(WINS // STEP_B,),
        in_specs=[
            pl.BlockSpec((STEP_B, 2 * CAP, BINS_B), lambda g: (g, 0, 0)),
            pl.BlockSpec((STEP_B, 2 * SRC, BINS_B), lambda g: (g, 0, BINS_A // BINS_B)),
            pl.BlockSpec((STEP_B, WIDE, SLOTS), lambda g: (g, 0, 0)),
        ],
        out_specs=pl.BlockSpec(shape, lambda g: (0, 0, 0)),
        out_shape=jax.ShapeDtypeStruct(shape, dtype),
        scratch_shapes=[
            pltpu.VMEM((STEP_B, WIDE, 2 * BINS_B), jnp.float32),
            pltpu.VMEM((STEP_B, 2 * SRC, BINS_B), jnp.float32),
            pltpu.VMEM(shape, jnp.float32),
        ],
        cost_estimate=pl.CostEstimate(flops=8_000_000_000, bytes_accessed=8_000_000, transcendentals=0),
        compiler_params=pltpu.CompilerParams(vmem_limit_bytes=32 << 20),
        name="cross_sums_second",
    )(got, source, picks)


def split(x):
    high = x.astype(jnp.bfloat16)
    return high, (x - high.astype(jnp.float32)).astype(jnp.bfloat16)


def three_dots(high, low, table_high, table_low):
    t = table_high[...]
    return dot(high[...], t) + (dot(low[...], t) + dot(high[...], table_low[...]))


def load_sums(mine, theirs, high, low):
    total = mine[...] + theirs[...].astype(jnp.float32)
    h, rest = split(total)
    high[...] = h
    low[...] = rest


def lags_first_kernel(mine, theirs, table_high, table_low, out, high, low):
    @pl.when(pl.program_id(0) == 0)
    def _():
        load_sums(mine, theirs, high, low)

    out[...] = three_dots(high, low, table_high, table_low)


def lags_last_kernel(mine, theirs, table_high, table_low, before, count, count_theirs, out, high, low, scale):
    @pl.when(pl.program_id(0) == 0)
    def _():
        load_sums(mine, theirs, high, low)
        for q in range(SB):
            pairs = count[:, SB + q : SB + q + 1] + count_theirs[:, q : q + 1]
            scale[q * WIDE : (q + 1) * WIDE] = jnp.broadcast_to(1.0 / jnp.maximum(pairs, 1.0), (WIDE, 128))

    out[...] = (before[...] + three_dots(high, low, table_high, table_low)) * scale[:, 0:1]


def to_lags(mine, theirs, tables, before=None, counts=()):
    rows, depth = SB * WIDE, tables[0].shape[0]
    tile = pl.BlockSpec((rows, LAG_TILE), lambda n: (0, n))
    full = lambda shape: pl.BlockSpec(shape, lambda n: (0, 0))
    table = pl.BlockSpec((depth, LAG_TILE), lambda n: (0, n))
    last = before is not None
    return pl.pallas_call(
        lags_last_kernel if last else lags_first_kernel,
        grid=(pl.cdiv(LAGS, LAG_TILE),),
        in_specs=[full((rows, depth)), full((rows, depth)), table, table]
        + ([tile, full((WIDE, 128)), full((WIDE, 128))] if last else []),
        out_specs=tile,
        out_shape=jax.ShapeDtypeStruct((rows, LAGS), jnp.float32),
        scratch_shapes=[pltpu.VMEM((rows, depth), jnp.bfloat16)] * 2
        + ([pltpu.VMEM((rows, 128), jnp.float32)] if last else []),
        cost_estimate=pl.CostEstimate(flops=6 * rows * depth * LAGS, bytes_accessed=4 * rows * LAGS * (2 if last else 1), transcendentals=0),
        compiler_params=pltpu.CompilerParams(vmem_limit_bytes=32 << 20),
        name="to_lags_last" if last else "to_lags_first",
    )(
        mine.reshape(rows, depth),
        theirs.reshape(rows, depth),
        *tables,
        *((before, *counts) if last else ()),
    )


def lag_table(first_bin, bins, zero):
    bin_index = F0 + first_bin + zero + jnp.arange(bins, dtype=jnp.int32)
    lag_index = jnp.arange(LAGS, dtype=jnp.int32) - MAXLAG
    phase_steps = jnp.mod(bin_index[:, None] * lag_index[None, :], NFFT)
    angles = phase_steps.astype(jnp.float32) * jnp.float32(2.0 * math.pi / NFFT)
    table = jnp.concatenate([jnp.cos(angles), -jnp.sin(angles)], axis=0)
    high = lax.reduce_precision(table, 8, 7)
    return high.astype(jnp.bfloat16), (table - high).astype(jnp.bfloat16)


def swap(x):
    return lax.ppermute(x, "tm", [(0, 1), (1, 0)])


def local(spectra, mask):
    tm_index = lax.axis_index("tm").astype(jnp.int32)[None]
    flags = mask.reshape(BLOCKS, WIDE)
    spectra = spectra.reshape(CH, 2, F)
    source = source_rows(tm_index, flags, spectra)
    gathered = lax.all_gather(source, "chan", axis=0, tiled=True)
    flags, _ = lax.optimization_barrier((flags, source))
    send_a, send_b = pack(flags, spectra)
    send_a, zero = lax.optimization_barrier((send_a, jnp.int32(0)))
    tables_a = lag_table(0, BINS_A, zero)
    tables_b = lag_table(BINS_A, BINS_B, zero)
    send_b, tables_a, tables_b = lax.optimization_barrier((send_b, tables_a, tables_b))
    exchange = lambda x: lax.all_to_all(x, "chan", split_axis=0, concat_axis=0, tiled=True)
    got_a = exchange(send_a)
    got_b = exchange(send_b)
    theirs_a, mine_a, picks, count = first_sums(got_a, gathered)
    from_a = swap(theirs_a)
    count_from = swap(count)
    lagged = to_lags(mine_a, from_a, tables_a)
    got_b, lagged = lax.optimization_barrier((got_b, lagged))
    theirs_b = second_sums(got_b, gathered, picks, 0, jnp.bfloat16)
    from_b = swap(theirs_b)
    mine_b = second_sums(got_b, gathered, picks, SB, jnp.float32)
    lagged = to_lags(mine_b, from_b, tables_b, lagged, (count, count_from))
    return lagged.reshape(SB, WIDE, LAGS)


def solution(mesh):
    placed = (P("tm", "chan", None, None, None), P("tm", "chan", None))
    return jax.shard_map(
        local, mesh=mesh, in_specs=placed, out_specs=P("tm", "chan", None), check_vma=False
    )
```

```python
import functools
import math

import jax
import jax.numpy as jnp
from jax import lax
from jax.experimental import pallas as pl
from jax.experimental.pallas import tpu as pltpu
from jax.sharding import PartitionSpec as P

CH = 10240
F = 384
F0 = 12
NFFT = 6000
MAXLAG = 1500
SB = 4
SRC = 8
LAGS = 3001
BLOCKS = 64
WIDE = 160
WINS = 64
SLOTS = 128
ROWS = 2 * SLOTS
BINS_A = 256
BINS_B = 128
CAP = 120
PACK = 8
GRANT = 56 << 20
STEP_A = 16
STEP_B = 16
LAG_TILE = 512


def iota(shape, dim):
    return lax.broadcasted_iota(jnp.int32, shape, dim)


def one_hot(where):
    return jnp.where(where, 1.0, 0.0).astype(jnp.bfloat16)


def dot(a, b):
    return jnp.dot(a, b, preferred_element_type=jnp.float32)


def source_kernel(tm_ref, mask_ref, a0, a1, a2, b0, b1, b2, out):
    middle = BLOCKS // 2
    flags = mask_ref[...].astype(jnp.float32).astype(jnp.bfloat16)
    shift = SB * (1 - tm_ref[0])
    lane = iota((WIDE, 128), 1)
    row = iota((WIDE, 128), 0)
    source = (lane + shift) % SRC
    first = dot(flags, one_hot((row == source % SB) & (source < SB) & (lane < SRC)))
    second = dot(flags, one_hot((row == source % SB) & (source >= SB) & (lane < SRC)))
    kept = dot(flags, one_hot(row == lane // 2))
    take = iota((2 * SRC, 16), 0)
    lane = iota((2 * SRC, 16), 1)
    source = (take % SRC + shift) % SRC
    hit = lane == 2 * (source % SB) + take // SRC
    pick_a = one_hot(hit & (source < SB) & (kept[0:1, :16] > 0.5))
    pick_b = one_hot(hit & (source >= SB) & (kept[middle : middle + 1, :16] > 0.5))
    rows = [
        dot(pick_a, ra.reshape(16, 128)[...]) + dot(pick_b, rb.reshape(16, 128)[...])
        for ra, rb in ((a0, b0), (a1, b1), (a2, b2))
    ]
    squares = sum(r * r for r in rows)
    energy = jnp.sum(squares[:SRC] + squares[SRC:], axis=1, keepdims=True) / F
    factor = lax.rsqrt(energy + 1e-06)
    factor = jnp.concatenate([factor, factor], axis=0)
    for k, r in enumerate(rows):
        out[0, :, k * 128 : (k + 1) * 128] = (r * factor).astype(jnp.bfloat16)
    line = iota((2 * SRC, 128), 0)
    flag_line = first[0:1] + second[middle : middle + 1]
    out[0, :, F:] = jnp.where(line == 0, flag_line, 0.0).astype(jnp.bfloat16)


def source_rows(tm_index, mask, spectra):
    head = lambda k, at: pl.BlockSpec((8, 2, 128), lambda i: (at, 0, k))
    middle = BLOCKS // 2 * WIDE // 8
    return pl.pallas_call(
        source_kernel,
        grid=(1,),
        in_specs=[
            pl.BlockSpec(memory_space=pltpu.SMEM),
            pl.BlockSpec((BLOCKS, WIDE), lambda i: (0, 0)),
            *[head(k, 0) for k in range(3)],
            *[head(k, middle) for k in range(3)],
        ],
        out_specs=pl.BlockSpec((1, 2 * SRC, F + 128), lambda i: (0, 0, 0)),
        out_shape=jax.ShapeDtypeStruct((1, 2 * SRC, F + 128), jnp.bfloat16),
        cost_estimate=pl.CostEstimate(flops=10_000_000, bytes_accessed=100_000, transcendentals=0),
        name="source_rows",
    )(tm_index, mask, *[spectra] * 6)


def pack_kernel(mask_ref, src_ref, x0, x1, x2, send_a, send_b, slot_ref, key_ref):
    step = pl.program_id(0)

    @pl.when(step == 0)
    def _():
        flags = mask_ref[...].astype(jnp.float32).astype(jnp.bfloat16)
        lane = iota((WIDE, 2 * WIDE), 1)
        row = iota((WIDE, 2 * WIDE), 0)
        before = dot(flags, one_hot(row < lane // 2))
        kept = dot(flags, one_hot(row == lane // 2))
        part = (iota((BLOCKS, 2 * WIDE), 1) % 2).astype(jnp.float32)
        slot_ref[...] = jnp.where(kept > 0.5, before + part * SLOTS, -1.0)
        lane = iota((WIDE, BINS_A), 1)
        row = iota((WIDE, BINS_A), 0)
        before = dot(flags, one_hot(row < lane))
        key_ref[...] = jnp.where(dot(flags, one_hot(row == lane)) > 0.5, before, -1.0)

    flag_line = src_ref[0, :1, F:].astype(jnp.float32)
    flag_line = jnp.concatenate([flag_line, flag_line], axis=1)
    place = iota((ROWS, 2 * WIDE), 0).astype(jnp.float32).astype(jnp.bfloat16)
    for n in range(PACK):
        block = step * PACK + n
        slot = slot_ref[pl.ds(block, 1), :].astype(jnp.bfloat16)
        pick = jnp.where(place == slot, jnp.ones_like(place), jnp.zeros_like(place))
        at = pl.ds(n * 2 * WIDE, 2 * WIDE)
        band = jnp.concatenate([r.reshape(PACK * 2 * WIDE, 128)[at, :] for r in (x0, x1, x2)], axis=1)
        rows = dot(pick, band)
        real, imag = rows[:CAP], rows[SLOTS : SLOTS + CAP]
        energy = jnp.sum(real * real + imag * imag, axis=1, keepdims=True) / F
        factor = lax.rsqrt(energy + 1e-06)
        real = (real * factor).astype(jnp.bfloat16)
        imag = (imag * factor).astype(jnp.bfloat16)
        for out, lo, hi in ((send_a, 0, BINS_A), (send_b, BINS_A, F)):
            out[n, :CAP] = real[:, lo:hi]
            out[n, CAP:SLOTS] = src_ref[0, :SRC, lo:hi]
            out[n, SLOTS : SLOTS + CAP] = imag[:, lo:hi]
            out[n, SLOTS + CAP : ROWS] = src_ref[0, SRC:, lo:hi]
        line = iota((8, BINS_A), 0)
        notes = jnp.where(line == 0, key_ref[pl.ds(block, 1), :], flag_line)
        send_a[n, ROWS:] = notes.astype(jnp.bfloat16)


def pack(mask, source, spectra):
    band = lambda k: pl.BlockSpec((PACK * WIDE, 2, 128), lambda b: (b, 0, k))
    return pl.pallas_call(
        pack_kernel,
        grid=(BLOCKS // PACK,),
        in_specs=[
            pl.BlockSpec((BLOCKS, WIDE), lambda b: (0, 0)),
            pl.BlockSpec((1, 2 * SRC, F + 128), lambda b: (0, 0, 0)),
            *[band(k) for k in range(3)],
        ],
        out_specs=[
            pl.BlockSpec((PACK, ROWS + 8, BINS_A), lambda b: (b, 0, 0)),
            pl.BlockSpec((PACK, ROWS, BINS_B), lambda b: (b, 0, 0)),
        ],
        out_shape=[
            jax.ShapeDtypeStruct((BLOCKS, ROWS + 8, BINS_A), jnp.bfloat16),
            jax.ShapeDtypeStruct((BLOCKS, ROWS, BINS_B), jnp.bfloat16),
        ],
        scratch_shapes=[
            pltpu.VMEM((BLOCKS, 2 * WIDE), jnp.float32),
            pltpu.VMEM((BLOCKS, BINS_A), jnp.float32),
        ],
        cost_estimate=pl.CostEstimate(flops=2 * BLOCKS * ROWS * 2 * WIDE * F, bytes_accessed=30_000_000, transcendentals=0),
        compiler_params=pltpu.CompilerParams(vmem_limit_bytes=GRANT),
        name="whiten_pack",
    )(mask, source, *[spectra] * 3)


def spread_slots(got, pick, held, src, win, bins):
    rows = jnp.concatenate([got[win, :SLOTS, :], got[win, SLOTS:ROWS, :]], axis=1)
    held[win] = dot(pick, rows)
    real = rows[CAP:, :bins].astype(jnp.float32)
    imag = rows[CAP:, bins:].astype(jnp.float32)
    src[win, :SRC] = real
    src[win, SRC : 2 * SRC] = imag
    src[win, 2 * SRC :] = real + imag


def correlate(held, src, total, sources, bins, steps):
    def group(i, _):
        rows = pl.ds(pl.multiple_of(i * 8, 8), 8)
        for t in range(0, bins, 128):
            lanes = [slice(k * bins + t, k * bins + t + 128) for k in range(3)]
            sums = [[total[n, rows, at] for at in lanes] for n in range(len(sources))]
            for win in range(steps):
                b0, b1 = held[win, rows, lanes[0]], held[win, rows, lanes[1]]
                for n, q in enumerate(sources):
                    for k, b in enumerate((b0, b1, b0 - b1)):
                        a = src[win, k * SRC + q : k * SRC + q + 1, lanes[0]]
                        sums[n][k] += jnp.broadcast_to(a, (8, 128)) * b
            for n in range(len(sources)):
                for at, value in zip(lanes, sums[n]):
                    total[n, rows, at] = value
        return 0

    lax.fori_loop(0, WIDE // 8, group, 0)


def store_sums(total, n, out, q, bins):
    p, m, r = (total[n, :, k * bins : (k + 1) * bins] for k in range(3))
    out[q, :, :bins] = (p + m).astype(out.dtype)
    out[q, :, bins:] = (r - p + m).astype(out.dtype)


def first_kernel(got, theirs, mine, picks, count, held, src, total):
    step = pl.program_id(0)

    @pl.when(step == 0)
    def _():
        total[...] = jnp.zeros_like(total)
        count[...] = jnp.zeros_like(count)

    for win in range(STEP_A):
        notes = got[win, ROWS:, :].astype(jnp.float32)
        key = jnp.transpose(notes)[:WIDE, 0:1]
        pick = one_hot(iota((WIDE, SLOTS), 1) == key.astype(jnp.int32))
        picks[win] = pick
        count[...] += jnp.where(key > -0.5, 1.0, 0.0) * notes[1:2, :128]
        spread_slots(got, pick, held, src, win, BINS_A)
    correlate(held, src, total, range(SRC), BINS_A, STEP_A)

    @pl.when(step == pl.num_programs(0) - 1)
    def _():
        for q in range(SB):
            store_sums(total, q, theirs, q, BINS_A)
            store_sums(total, SB + q, mine, q, BINS_A)


def first_sums(got):
    shape = (SB, WIDE, 2 * BINS_A)
    sums_spec = pl.BlockSpec(shape, lambda g: (0, 0, 0))
    return pl.pallas_call(
        first_kernel,
        grid=(WINS // STEP_A,),
        in_specs=[pl.BlockSpec((STEP_A, ROWS + 8, BINS_A), lambda g: (g, 0, 0))],
        out_specs=[
            sums_spec,
            sums_spec,
            pl.BlockSpec((STEP_A, WIDE, SLOTS), lambda g: (g, 0, 0)),
            pl.BlockSpec((WIDE, 128), lambda g: (0, 0)),
        ],
        out_shape=[
            jax.ShapeDtypeStruct(shape, jnp.bfloat16),
            jax.ShapeDtypeStruct(shape, jnp.float32),
            jax.ShapeDtypeStruct((WINS, WIDE, SLOTS), jnp.bfloat16),
            jax.ShapeDtypeStruct((WIDE, 128), jnp.float32),
        ],
        scratch_shapes=[
            pltpu.VMEM((STEP_A, WIDE, 2 * BINS_A), jnp.float32),
            pltpu.VMEM((STEP_A, 3 * SRC, BINS_A), jnp.float32),
            pltpu.VMEM((SRC, WIDE, 3 * BINS_A), jnp.float32),
        ],
        cost_estimate=pl.CostEstimate(flops=30_000_000_000, bytes_accessed=20_000_000, transcendentals=0),
        compiler_params=pltpu.CompilerParams(vmem_limit_bytes=GRANT),
        name="cross_sums_first",
    )(got)


def second_kernel(first, got, picks, out, held, src, total):
    step = pl.program_id(0)

    @pl.when(step == 0)
    def _():
        total[...] = jnp.zeros_like(total)

    for win in range(STEP_B):
        spread_slots(got, picks[win], held, src, win, BINS_B)
    correlate(held, src, total, range(first, first + SB), BINS_B, STEP_B)

    @pl.when(step == pl.num_programs(0) - 1)
    def _():
        for q in range(SB):
            store_sums(total, q, out, q, BINS_B)


def second_sums(got, picks, first, dtype):
    shape = (SB, WIDE, 2 * BINS_B)
    return pl.pallas_call(
        functools.partial(second_kernel, first),
        grid=(WINS // STEP_B,),
        in_specs=[
            pl.BlockSpec((STEP_B, ROWS, BINS_B), lambda g: (g, 0, 0)),
            pl.BlockSpec((STEP_B, WIDE, SLOTS), lambda g: (g, 0, 0)),
        ],
        out_specs=pl.BlockSpec(shape, lambda g: (0, 0, 0)),
        out_shape=jax.ShapeDtypeStruct(shape, dtype),
        scratch_shapes=[
            pltpu.VMEM((STEP_B, WIDE, 2 * BINS_B), jnp.float32),
            pltpu.VMEM((STEP_B, 3 * SRC, BINS_B), jnp.float32),
            pltpu.VMEM((SB, WIDE, 3 * BINS_B), jnp.float32),
        ],
        cost_estimate=pl.CostEstimate(flops=8_000_000_000, bytes_accessed=8_000_000, transcendentals=0),
        compiler_params=pltpu.CompilerParams(vmem_limit_bytes=GRANT),
        name="cross_sums_second",
    )(got, picks)


def split(x):
    high = x.astype(jnp.bfloat16)
    return high, (x - high.astype(jnp.float32)).astype(jnp.bfloat16)


def three_dots(high, low, table_high, table_low):
    t = table_high[...]
    return dot(high[...], t) + (dot(low[...], t) + dot(high[...], table_low[...]))


def load_sums(mine, theirs, high, low):
    total = mine[...] + theirs[...].astype(jnp.float32)
    h, rest = split(total)
    high[...] = h
    low[...] = rest


def lags_first_kernel(mine, theirs, table_high, table_low, out, high, low):
    @pl.when(pl.program_id(0) == 0)
    def _():
        load_sums(mine, theirs, high, low)

    out[...] = three_dots(high, low, table_high, table_low)


def lags_last_kernel(mine, theirs, table_high, table_low, before, count, count_theirs, out, high, low, scale):
    @pl.when(pl.program_id(0) == 0)
    def _():
        load_sums(mine, theirs, high, low)
        for q in range(SB):
            pairs = count[:, SB + q : SB + q + 1] + count_theirs[:, q : q + 1]
            scale[q * WIDE : (q + 1) * WIDE] = jnp.broadcast_to(1.0 / jnp.maximum(pairs, 1.0), (WIDE, 128))

    out[...] = (before[...] + three_dots(high, low, table_high, table_low)) * scale[:, 0:1]


def to_lags(mine, theirs, tables, before=None, counts=()):
    rows, depth = SB * WIDE, tables[0].shape[0]
    tile = pl.BlockSpec((rows, LAG_TILE), lambda n: (0, n))
    full = lambda shape: pl.BlockSpec(shape, lambda n: (0, 0))
    table = pl.BlockSpec((depth, LAG_TILE), lambda n: (0, n))
    last = before is not None
    return pl.pallas_call(
        lags_last_kernel if last else lags_first_kernel,
        grid=(pl.cdiv(LAGS, LAG_TILE),),
        in_specs=[full((rows, depth)), full((rows, depth)), table, table]
        + ([tile, full((WIDE, 128)), full((WIDE, 128))] if last else []),
        out_specs=tile,
        out_shape=jax.ShapeDtypeStruct((rows, LAGS), jnp.float32),
        scratch_shapes=[pltpu.VMEM((rows, depth), jnp.bfloat16)] * 2
        + ([pltpu.VMEM((rows, 128), jnp.float32)] if last else []),
        cost_estimate=pl.CostEstimate(flops=6 * rows * depth * LAGS, bytes_accessed=4 * rows * LAGS * (2 if last else 1), transcendentals=0),
        compiler_params=pltpu.CompilerParams(vmem_limit_bytes=GRANT // 2 if last else GRANT),
        name="to_lags_last" if last else "to_lags_first",
    )(
        mine.reshape(rows, depth),
        theirs.reshape(rows, depth),
        *tables,
        *((before, *counts) if last else ()),
    )


def lag_table(first_bin, bins, zero):
    bin_index = F0 + first_bin + zero + jnp.arange(bins, dtype=jnp.int32)
    lag_index = jnp.arange(LAGS, dtype=jnp.int32) - MAXLAG
    phase_steps = jnp.mod(bin_index[:, None] * lag_index[None, :], NFFT)
    angles = phase_steps.astype(jnp.float32) * jnp.float32(2.0 * math.pi / NFFT)
    table = jnp.concatenate([jnp.cos(angles), -jnp.sin(angles)], axis=0)
    high = lax.reduce_precision(table, 8, 7)
    return high.astype(jnp.bfloat16), (table - high).astype(jnp.bfloat16)


def swap(x):
    return lax.ppermute(x, "tm", [(0, 1), (1, 0)])


def local(spectra, mask):
    tm_index = lax.axis_index("tm").astype(jnp.int32)[None]
    flags = mask.reshape(BLOCKS, WIDE)
    spectra = spectra.reshape(CH, 2, F)
    source = source_rows(tm_index, flags, spectra)
    send_a, send_b = pack(flags, source, spectra)
    send_a, zero = lax.optimization_barrier((send_a, jnp.int32(0)))
    tables_a = lag_table(0, BINS_A, zero)
    tables_b = lag_table(BINS_A, BINS_B, zero)
    send_b, tables_a, tables_b = lax.optimization_barrier((send_b, tables_a, tables_b))
    exchange = lambda x: lax.all_to_all(x, "chan", split_axis=0, concat_axis=0, tiled=True)
    got_a = exchange(send_a)
    got_b = exchange(send_b)
    theirs_a, mine_a, picks, count = first_sums(got_a)
    from_a = swap(theirs_a)
    count_from = swap(count)
    lagged = to_lags(mine_a, from_a, tables_a)
    got_b, lagged = lax.optimization_barrier((got_b, lagged))
    theirs_b = second_sums(got_b, picks, 0, jnp.bfloat16)
    from_b = swap(theirs_b)
    mine_b = second_sums(got_b, picks, SB, jnp.float32)
    lagged = to_lags(mine_b, from_b, tables_b, lagged, (count, count_from))
    return lagged.reshape(SB, WIDE, LAGS)


def solution(mesh):
    placed = (P("tm", "chan", None, None, None), P("tm", "chan", None))
    return jax.shard_map(
        local, mesh=mesh, in_specs=placed, out_specs=P("tm", "chan", None), check_vma=False
    )
```

```python
import functools
import math

import jax
import jax.numpy as jnp
from jax import lax
from jax.experimental import pallas as pl
from jax.experimental.pallas import tpu as pltpu
from jax.sharding import PartitionSpec as P

CH = 10240
F = 384
F0 = 12
NFFT = 6000
MAXLAG = 1500
SB = 4
SRC = 8
LAGS = 3001
BLOCKS = 64
WIDE = 160
WINS = 64
SLOTS = 128
ROWS = 2 * SLOTS
BINS_A = 256
BINS_B = 128
CAP = 120
PACK = 8
GRANT = 56 << 20
LAG_GRANT = 44 << 20
STEP_A = 16
STEP_B = 16
TALL = 32
LAG_TILE = 1024


def iota(shape, dim):
    return lax.broadcasted_iota(jnp.int32, shape, dim)


def one_hot(where):
    return jnp.where(where, 1.0, 0.0).astype(jnp.bfloat16)


def dot(a, b):
    return jnp.dot(a, b, preferred_element_type=jnp.float32)


def source_kernel(tm_ref, mask_ref, a0, a1, a2, b0, b1, b2, out):
    middle = BLOCKS // 2
    flags = mask_ref[...].astype(jnp.float32).astype(jnp.bfloat16)
    shift = SB * (1 - tm_ref[0])
    lane = iota((WIDE, 128), 1)
    row = iota((WIDE, 128), 0)
    source = (lane + shift) % SRC
    first = dot(flags, one_hot((row == source % SB) & (source < SB) & (lane < SRC)))
    second = dot(flags, one_hot((row == source % SB) & (source >= SB) & (lane < SRC)))
    kept = dot(flags, one_hot(row == lane // 2))
    take = iota((2 * SRC, 16), 0)
    lane = iota((2 * SRC, 16), 1)
    source = (take % SRC + shift) % SRC
    hit = lane == 2 * (source % SB) + take // SRC
    pick_a = one_hot(hit & (source < SB) & (kept[0:1, :16] > 0.5))
    pick_b = one_hot(hit & (source >= SB) & (kept[middle : middle + 1, :16] > 0.5))
    rows = [
        dot(pick_a, ra.reshape(16, 128)[...]) + dot(pick_b, rb.reshape(16, 128)[...])
        for ra, rb in ((a0, b0), (a1, b1), (a2, b2))
    ]
    squares = sum(r * r for r in rows)
    energy = jnp.sum(squares[:SRC] + squares[SRC:], axis=1, keepdims=True) / F
    factor = lax.rsqrt(energy + 1e-06)
    factor = jnp.concatenate([factor, factor], axis=0)
    for k, r in enumerate(rows):
        out[0, :, k * 128 : (k + 1) * 128] = (r * factor).astype(jnp.bfloat16)
    line = iota((2 * SRC, 128), 0)
    flag_line = first[0:1] + second[middle : middle + 1]
    out[0, :, F:] = jnp.where(line == 0, flag_line, 0.0).astype(jnp.bfloat16)


def source_rows(tm_index, mask, spectra):
    head = lambda k, at: pl.BlockSpec((8, 2, 128), lambda i: (at, 0, k))
    middle = BLOCKS // 2 * WIDE // 8
    return pl.pallas_call(
        source_kernel,
        grid=(1,),
        in_specs=[
            pl.BlockSpec(memory_space=pltpu.SMEM),
            pl.BlockSpec((BLOCKS, WIDE), lambda i: (0, 0)),
            *[head(k, 0) for k in range(3)],
            *[head(k, middle) for k in range(3)],
        ],
        out_specs=pl.BlockSpec((1, 2 * SRC, F + 128), lambda i: (0, 0, 0)),
        out_shape=jax.ShapeDtypeStruct((1, 2 * SRC, F + 128), jnp.bfloat16),
        cost_estimate=pl.CostEstimate(flops=10_000_000, bytes_accessed=100_000, transcendentals=0),
        name="source_rows",
    )(tm_index, mask, *[spectra] * 6)


def pack_kernel(mask_ref, src_ref, x0, x1, x2, send_a, send_b, slot_ref, key_ref):
    step = pl.program_id(0)

    @pl.when(step == 0)
    def _():
        flags = mask_ref[...].astype(jnp.float32).astype(jnp.bfloat16)
        lane = iota((WIDE, 2 * WIDE), 1)
        row = iota((WIDE, 2 * WIDE), 0)
        before = dot(flags, one_hot(row < lane // 2))
        kept = dot(flags, one_hot(row == lane // 2))
        part = (iota((BLOCKS, 2 * WIDE), 1) % 2).astype(jnp.float32)
        slot_ref[...] = jnp.where(kept > 0.5, before + part * SLOTS, -1.0)
        lane = iota((WIDE, BINS_A), 1)
        row = iota((WIDE, BINS_A), 0)
        before = dot(flags, one_hot(row < lane))
        key_ref[...] = jnp.where(dot(flags, one_hot(row == lane)) > 0.5, before, -1.0)

    flag_line = src_ref[0, :1, F:].astype(jnp.float32)
    flag_line = jnp.concatenate([flag_line, flag_line], axis=1)
    place = iota((ROWS, 2 * WIDE), 0).astype(jnp.float32).astype(jnp.bfloat16)
    for n in range(PACK):
        block = step * PACK + n
        slot = slot_ref[pl.ds(block, 1), :].astype(jnp.bfloat16)
        pick = jnp.where(place == slot, jnp.ones_like(place), jnp.zeros_like(place))
        at = pl.ds(n * 2 * WIDE, 2 * WIDE)
        band = jnp.concatenate([r.reshape(PACK * 2 * WIDE, 128)[at, :] for r in (x0, x1, x2)], axis=1)
        rows = dot(pick, band)
        real, imag = rows[:CAP], rows[SLOTS : SLOTS + CAP]
        energy = jnp.sum(real * real + imag * imag, axis=1, keepdims=True) / F
        factor = lax.rsqrt(energy + 1e-06)
        real = (real * factor).astype(jnp.bfloat16)
        imag = (imag * factor).astype(jnp.bfloat16)
        for out, lo, hi in ((send_a, 0, BINS_A), (send_b, BINS_A, F)):
            out[n, :CAP] = real[:, lo:hi]
            out[n, CAP:SLOTS] = src_ref[0, :SRC, lo:hi]
            out[n, SLOTS : SLOTS + CAP] = imag[:, lo:hi]
            out[n, SLOTS + CAP : ROWS] = src_ref[0, SRC:, lo:hi]
        line = iota((8, BINS_A), 0)
        notes = jnp.where(line == 0, key_ref[pl.ds(block, 1), :], flag_line)
        send_a[n, ROWS:] = notes.astype(jnp.bfloat16)


def pack(mask, source, spectra):
    band = lambda k: pl.BlockSpec((PACK * WIDE, 2, 128), lambda b: (b, 0, k))
    return pl.pallas_call(
        pack_kernel,
        grid=(BLOCKS // PACK,),
        in_specs=[
            pl.BlockSpec((BLOCKS, WIDE), lambda b: (0, 0)),
            pl.BlockSpec((1, 2 * SRC, F + 128), lambda b: (0, 0, 0)),
            *[band(k) for k in range(3)],
        ],
        out_specs=[
            pl.BlockSpec((PACK, ROWS + 8, BINS_A), lambda b: (b, 0, 0)),
            pl.BlockSpec((PACK, ROWS, BINS_B), lambda b: (b, 0, 0)),
        ],
        out_shape=[
            jax.ShapeDtypeStruct((BLOCKS, ROWS + 8, BINS_A), jnp.bfloat16),
            jax.ShapeDtypeStruct((BLOCKS, ROWS, BINS_B), jnp.bfloat16),
        ],
        scratch_shapes=[
            pltpu.VMEM((BLOCKS, 2 * WIDE), jnp.float32),
            pltpu.VMEM((BLOCKS, BINS_A), jnp.float32),
        ],
        cost_estimate=pl.CostEstimate(flops=2 * BLOCKS * ROWS * 2 * WIDE * F, bytes_accessed=30_000_000, transcendentals=0),
        compiler_params=pltpu.CompilerParams(vmem_limit_bytes=GRANT),
        name="whiten_pack",
    )(mask, source, *[spectra] * 3)


def spread_slots(got, pick, held, src, win, bins):
    rows = jnp.concatenate([got[win, :SLOTS, :], got[win, SLOTS:ROWS, :]], axis=1)
    held[win] = dot(pick, rows)
    real = rows[CAP:, :bins].astype(jnp.float32)
    imag = rows[CAP:, bins:].astype(jnp.float32)
    for k, rows in enumerate((real, imag, real + imag)):
        for t in range(bins // 128):
            src[win, t, k * SRC : (k + 1) * SRC] = rows[:, t * 128 : (t + 1) * 128]


def correlate(held, src, total, sources, bins, steps):
    def group(i, _):
        rows = [pl.ds(pl.multiple_of(i * TALL + r, 8), 8) for r in range(0, TALL, 8)]
        for t in range(0, bins, 128):
            lanes = [slice(k * bins + t, k * bins + t + 128) for k in range(3)]
            for some in range(0, len(sources), SB):
                sums = [[[total[some + n, row, at] for row in rows] for at in lanes] for n in range(SB)]
                for win in range(steps):
                    real = [held[win, row, lanes[0]] for row in rows]
                    imag = [held[win, row, lanes[1]] for row in rows]
                    less = [x - y for x, y in zip(real, imag)]
                    for n in range(SB):
                        for k, values in enumerate((real, imag, less)):
                            a = src[win, t // 128, pl.ds(k * SRC + sources[some + n], 8, stride=0), :]
                            for r, b in enumerate(values):
                                sums[n][k][r] += a * b
                for n in range(SB):
                    for k, at in enumerate(lanes):
                        for r, row in enumerate(rows):
                            total[some + n, row, at] = sums[n][k][r]
        return 0

    lax.fori_loop(0, WIDE // TALL, group, 0)


def store_sums(total, n, out, q, bins):
    p, m, r = (total[n, :, k * bins : (k + 1) * bins] for k in range(3))
    out[q, :, :bins] = (p + m).astype(out.dtype)
    out[q, :, bins:] = (r - p + m).astype(out.dtype)


def first_kernel(got, theirs, mine, picks, count, held, src, total):
    step = pl.program_id(0)

    @pl.when(step == 0)
    def _():
        total[...] = jnp.zeros_like(total)
        count[...] = jnp.zeros_like(count)

    for win in range(STEP_A):
        notes = got[win, ROWS:, :].astype(jnp.float32)
        key = jnp.transpose(notes)[:WIDE, 0:1]
        pick = one_hot(iota((WIDE, SLOTS), 1) == key.astype(jnp.int32))
        picks[win] = pick
        count[...] += jnp.where(key > -0.5, 1.0, 0.0) * notes[1:2, :128]
        spread_slots(got, pick, held, src, win, BINS_A)
    correlate(held, src, total, range(SRC), BINS_A, STEP_A)

    @pl.when(step == pl.num_programs(0) - 1)
    def _():
        for q in range(SB):
            store_sums(total, q, theirs, q, BINS_A)
            store_sums(total, SB + q, mine, q, BINS_A)


def first_sums(got):
    shape = (SB, WIDE, 2 * BINS_A)
    sums_spec = pl.BlockSpec(shape, lambda g: (0, 0, 0))
    return pl.pallas_call(
        first_kernel,
        grid=(WINS // STEP_A,),
        in_specs=[pl.BlockSpec((STEP_A, ROWS + 8, BINS_A), lambda g: (g, 0, 0))],
        out_specs=[
            sums_spec,
            sums_spec,
            pl.BlockSpec((STEP_A, WIDE, SLOTS), lambda g: (g, 0, 0)),
            pl.BlockSpec((WIDE, 128), lambda g: (0, 0)),
        ],
        out_shape=[
            jax.ShapeDtypeStruct(shape, jnp.bfloat16),
            jax.ShapeDtypeStruct(shape, jnp.float32),
            jax.ShapeDtypeStruct((WINS, WIDE, SLOTS), jnp.bfloat16),
            jax.ShapeDtypeStruct((WIDE, 128), jnp.float32),
        ],
        scratch_shapes=[
            pltpu.VMEM((STEP_A, WIDE, 2 * BINS_A), jnp.float32),
            pltpu.VMEM((STEP_A, BINS_A // 128, 3 * SRC, 128), jnp.float32),
            pltpu.VMEM((SRC, WIDE, 3 * BINS_A), jnp.float32),
        ],
        cost_estimate=pl.CostEstimate(flops=30_000_000_000, bytes_accessed=20_000_000, transcendentals=0),
        compiler_params=pltpu.CompilerParams(vmem_limit_bytes=GRANT),
        name="cross_sums_first",
    )(got)


def second_kernel(first, got, picks, out, held, src, total):
    step = pl.program_id(0)

    @pl.when(step == 0)
    def _():
        total[...] = jnp.zeros_like(total)

    for win in range(STEP_B):
        spread_slots(got, picks[win], held, src, win, BINS_B)
    correlate(held, src, total, range(first, first + SB), BINS_B, STEP_B)

    @pl.when(step == pl.num_programs(0) - 1)
    def _():
        for q in range(SB):
            store_sums(total, q, out, q, BINS_B)


def second_sums(got, picks, first, dtype):
    shape = (SB, WIDE, 2 * BINS_B)
    return pl.pallas_call(
        functools.partial(second_kernel, first),
        grid=(WINS // STEP_B,),
        in_specs=[
            pl.BlockSpec((STEP_B, ROWS, BINS_B), lambda g: (g, 0, 0)),
            pl.BlockSpec((STEP_B, WIDE, SLOTS), lambda g: (g, 0, 0)),
        ],
        out_specs=pl.BlockSpec(shape, lambda g: (0, 0, 0)),
        out_shape=jax.ShapeDtypeStruct(shape, dtype),
        scratch_shapes=[
            pltpu.VMEM((STEP_B, WIDE, 2 * BINS_B), jnp.float32),
            pltpu.VMEM((STEP_B, BINS_B // 128, 3 * SRC, 128), jnp.float32),
            pltpu.VMEM((SB, WIDE, 3 * BINS_B), jnp.float32),
        ],
        cost_estimate=pl.CostEstimate(flops=8_000_000_000, bytes_accessed=8_000_000, transcendentals=0),
        compiler_params=pltpu.CompilerParams(vmem_limit_bytes=GRANT),
        name="cross_sums_second",
    )(got, picks)


def lags_kernel(mine_a, from_a, mine_b, from_b, table, count, count_from, out, held, scale):
    @pl.when(pl.program_id(0) == 0)
    def _():
        for mine, got, at in ((mine_a, from_a, slice(0, 2 * BINS_A)), (mine_b, from_b, slice(2 * BINS_A, 2 * F))):
            held[:, at] = (mine[...] + got[...].astype(jnp.float32)).astype(jnp.bfloat16)
        for q in range(SB):
            pairs = count[:, SB + q : SB + q + 1] + count_from[:, q : q + 1]
            scale[q * WIDE : (q + 1) * WIDE] = jnp.broadcast_to(1.0 / jnp.maximum(pairs, 1.0), (WIDE, 128))

    out[...] = dot(held[...], table[...]) * scale[:, 0:1]


def to_lags(mine_a, from_a, mine_b, from_b, table, count, count_from):
    rows = SB * WIDE
    full = lambda shape: pl.BlockSpec(shape, lambda n: (0, 0))
    sums = [full((rows, 2 * bins)) for bins in (BINS_A, BINS_A, BINS_B, BINS_B)]
    tiled = pl.BlockSpec((2 * F, LAG_TILE), lambda n: (0, n))
    return pl.pallas_call(
        lags_kernel,
        grid=(pl.cdiv(LAGS, LAG_TILE),),
        in_specs=[*sums, tiled, full((WIDE, 128)), full((WIDE, 128))],
        out_specs=pl.BlockSpec((rows, LAG_TILE), lambda n: (0, n)),
        out_shape=jax.ShapeDtypeStruct((rows, LAGS), jnp.float32),
        scratch_shapes=[
            pltpu.VMEM((rows, 2 * F), jnp.bfloat16),
            pltpu.VMEM((rows, 128), jnp.float32),
        ],
        cost_estimate=pl.CostEstimate(flops=4 * rows * F * LAGS, bytes_accessed=4 * rows * LAGS * 2, transcendentals=0),
        compiler_params=pltpu.CompilerParams(vmem_limit_bytes=LAG_GRANT),
        name="to_lags",
    )(*(x.reshape(rows, -1) for x in (mine_a, from_a, mine_b, from_b)), table, count, count_from)


def lag_table(zero):
    row = jnp.arange(2 * F, dtype=jnp.int32) + zero
    last = row >= 2 * BINS_A
    bins = jnp.where(last, BINS_B, BINS_A)
    inside = jnp.where(last, row - 2 * BINS_A, row)
    bin_index = F0 + jnp.where(last, BINS_A, 0) + inside % bins
    lag_index = jnp.arange(LAGS, dtype=jnp.int32) - MAXLAG
    phase_steps = jnp.mod(bin_index[:, None] * lag_index[None, :], NFFT)
    angles = phase_steps.astype(jnp.float32) * jnp.float32(2.0 * math.pi / NFFT)
    table = jnp.where((inside < bins)[:, None], jnp.cos(angles), -jnp.sin(angles))
    return table.astype(jnp.bfloat16)


def swap(x):
    return lax.ppermute(x, "tm", [(0, 1), (1, 0)])


def local(spectra, mask):
    tm_index = lax.axis_index("tm").astype(jnp.int32)[None]
    flags = mask.reshape(BLOCKS, WIDE)
    spectra = spectra.reshape(CH, 2, F)
    source = source_rows(tm_index, flags, spectra)
    send_a, send_b = pack(flags, source, spectra)
    send_a, zero = lax.optimization_barrier((send_a, jnp.int32(0)))
    table = lag_table(zero)
    send_b, table = lax.optimization_barrier((send_b, table))
    exchange = lambda x: lax.all_to_all(x, "chan", split_axis=0, concat_axis=0, tiled=True)
    got_a = exchange(send_a)
    got_b = exchange(send_b)
    theirs_a, mine_a, picks, count = first_sums(got_a)
    from_a = swap(theirs_a)
    count_from = swap(count)
    theirs_b = second_sums(got_b, picks, 0, jnp.bfloat16)
    from_b = swap(theirs_b)
    mine_b = second_sums(got_b, picks, SB, jnp.float32)
    lagged = to_lags(mine_a, from_a, mine_b, from_b, table, count, count_from)
    return lagged.reshape(SB, WIDE, LAGS)


def solution(mesh):
    placed = (P("tm", "chan", None, None, None), P("tm", "chan", None))
    return jax.shard_map(
        local, mesh=mesh, in_specs=placed, out_specs=P("tm", "chan", None), check_vma=False
    )
```

```python
import functools
import math

import jax
import jax.numpy as jnp
from jax import lax
from jax.experimental import pallas as pl
from jax.experimental.pallas import tpu as pltpu
from jax.sharding import PartitionSpec as P

CH = 10240
F = 384
F0 = 12
NFFT = 6000
MAXLAG = 1500
SB = 4
SRC = 8
LAGS = 3001
BLOCKS = 64
WIDE = 160
WINS = 64
LINES = 80
SLOTS = 128
ROWS = 2 * SLOTS
BINS_A = 256
BINS_B = 128
CAP = 120
PACK = 8
GRANT = 56 << 20
LAG_GRANT = 44 << 20
STEP_A = 16
STEP_B = 16
TALL = 32
LAG_TILE = 1024


def iota(shape, dim):
    return lax.broadcasted_iota(jnp.int32, shape, dim)


def one_hot(where):
    return jnp.where(where, 1.0, 0.0).astype(jnp.bfloat16)


def dot(a, b):
    return jnp.dot(a, b, preferred_element_type=jnp.float32)


def source_kernel(tm_ref, mask_ref, a0, a1, a2, b0, b1, b2, out, flag_out):
    middle = LINES // 2
    shift = SB * (1 - tm_ref[0])
    ones = lambda at: jnp.broadcast_to(mask_ref[at : at + 1, :], (16, 128)).astype(jnp.float32).astype(jnp.bfloat16)
    flags_a, flags_b = ones(0), ones(middle)
    lane = iota((128, 128), 1)
    row = iota((128, 128), 0)
    source = (lane + shift) % SRC
    here = (row == source % SB) & (lane < SRC)
    flag_out[...] = (dot(flags_a, one_hot(here & (source < SB))) + dot(flags_b, one_hot(here & (source >= SB))))[:8]
    twice = one_hot(row == lane // 2)
    kept_a, kept_b = dot(flags_a, twice), dot(flags_b, twice)
    take = iota((2 * SRC, 16), 0)
    lane = iota((2 * SRC, 16), 1)
    source = (take % SRC + shift) % SRC
    hit = lane == 2 * (source % SB) + take // SRC
    pick_a = one_hot(hit & (source < SB) & (kept_a[:, :16] > 0.5))
    pick_b = one_hot(hit & (source >= SB) & (kept_b[:, :16] > 0.5))
    rows = [
        dot(pick_a, ra.reshape(16, 128)[...]) + dot(pick_b, rb.reshape(16, 128)[...])
        for ra, rb in ((a0, b0), (a1, b1), (a2, b2))
    ]
    squares = sum(r * r for r in rows)
    energy = jnp.sum(squares[:SRC] + squares[SRC:], axis=1, keepdims=True) / F
    factor = lax.rsqrt(energy + 1e-06)
    factor = jnp.concatenate([factor, factor], axis=0)
    for k, r in enumerate(rows):
        out[0, :, k * 128 : (k + 1) * 128] = (r * factor).astype(jnp.bfloat16)


def source_rows(tm_index, mask, spectra):
    head = lambda k, at: pl.BlockSpec((8, 2, 128), lambda i: (at, 0, k))
    middle = BLOCKS // 2 * WIDE // 8
    return pl.pallas_call(
        source_kernel,
        grid=(1,),
        in_specs=[
            pl.BlockSpec(memory_space=pltpu.SMEM),
            pl.BlockSpec((LINES, 128), lambda i: (0, 0)),
            *[head(k, 0) for k in range(3)],
            *[head(k, middle) for k in range(3)],
        ],
        out_specs=[
            pl.BlockSpec((1, 2 * SRC, F), lambda i: (0, 0, 0)),
            pl.BlockSpec((8, 128), lambda i: (0, 0)),
        ],
        out_shape=[
            jax.ShapeDtypeStruct((1, 2 * SRC, F), jnp.bfloat16),
            jax.ShapeDtypeStruct((8, 128), jnp.float32),
        ],
        cost_estimate=pl.CostEstimate(flops=10_000_000, bytes_accessed=100_000, transcendentals=0),
        name="source_rows",
    )(tm_index, mask, *[spectra] * 6)


def pack_kernel(mask_ref, flag_ref, x0, x1, x2, send_a, send_b, slot_ref, key_ref):
    step = pl.program_id(0)

    @pl.when(step == 0)
    def _():
        lines = [mask_ref[pl.ds(k, LINES // 5, stride=5), :] for k in range(5)]
        lines = jnp.concatenate(lines, axis=1).astype(jnp.float32)
        lane = iota((WIDE, 2 * WIDE), 1)
        row = iota((WIDE, 2 * WIDE), 0)
        ahead_two, here_two = one_hot(row < lane // 2), one_hot(row == lane // 2)
        part = (iota((LINES // 5, 2 * WIDE), 1) % 2).astype(jnp.float32)
        lane = iota((WIDE, BINS_A), 1)
        row = iota((WIDE, BINS_A), 0)
        ahead, here = one_hot(row < lane), one_hot(row == lane)
        for m in range(4):
            flags = lines[:, m * WIDE : (m + 1) * WIDE].astype(jnp.bfloat16)
            slot_ref[m] = jnp.where(dot(flags, here_two) > 0.5, dot(flags, ahead_two) + part * SLOTS, -1.0)
            key_ref[m] = jnp.where(dot(flags, here) > 0.5, dot(flags, ahead), -1.0)

    flag_line = flag_ref[:1, :]
    flag_line = jnp.concatenate([flag_line, flag_line], axis=1)
    place = iota((ROWS, 2 * WIDE), 0).astype(jnp.float32).astype(jnp.bfloat16)
    for n in range(PACK):
        four = pl.ds(step * (PACK // 4) + n // 4, 1)
        slot = slot_ref[n % 4, four, :].astype(jnp.bfloat16)
        pick = jnp.where(place == slot, jnp.ones_like(place), jnp.zeros_like(place))
        at = pl.ds(n * 2 * WIDE, 2 * WIDE)
        band = jnp.concatenate([r.reshape(PACK * 2 * WIDE, 128)[at, :] for r in (x0, x1, x2)], axis=1)
        rows = dot(pick, band)
        real, imag = rows[:CAP], rows[SLOTS : SLOTS + CAP]
        energy = jnp.sum(real * real + imag * imag, axis=1, keepdims=True) / F
        factor = lax.rsqrt(energy + 1e-06)
        real = (real * factor).astype(jnp.bfloat16)
        imag = (imag * factor).astype(jnp.bfloat16)
        send_a[n, :CAP] = real[:, :BINS_A]
        line = iota((8, BINS_A), 0)
        notes = jnp.where(line == 0, key_ref[n % 4, four, :], flag_line)
        send_a[n, CAP:SLOTS] = notes.astype(jnp.bfloat16)
        send_a[n, SLOTS:] = imag[:, :BINS_A]
        send_b[n, :CAP] = real[:, BINS_A:]
        send_b[n, CAP:] = imag[:, BINS_A:]


def pack(mask, flags, spectra):
    band = lambda k: pl.BlockSpec((PACK * WIDE, 2, 128), lambda b: (b, 0, k))
    return pl.pallas_call(
        pack_kernel,
        grid=(BLOCKS // PACK,),
        in_specs=[
            pl.BlockSpec((LINES, 128), lambda b: (0, 0)),
            pl.BlockSpec((8, 128), lambda b: (0, 0)),
            *[band(k) for k in range(3)],
        ],
        out_specs=[
            pl.BlockSpec((PACK, SLOTS + CAP, BINS_A), lambda b: (b, 0, 0)),
            pl.BlockSpec((PACK, 2 * CAP, BINS_B), lambda b: (b, 0, 0)),
        ],
        out_shape=[
            jax.ShapeDtypeStruct((BLOCKS, SLOTS + CAP, BINS_A), jnp.bfloat16),
            jax.ShapeDtypeStruct((BLOCKS, 2 * CAP, BINS_B), jnp.bfloat16),
        ],
        scratch_shapes=[
            pltpu.VMEM((4, BLOCKS // 4, 2 * WIDE), jnp.float32),
            pltpu.VMEM((4, BLOCKS // 4, BINS_A), jnp.float32),
        ],
        cost_estimate=pl.CostEstimate(flops=2 * BLOCKS * ROWS * 2 * WIDE * F, bytes_accessed=30_000_000, transcendentals=0),
        compiler_params=pltpu.CompilerParams(vmem_limit_bytes=GRANT),
        name="whiten_pack",
    )(mask, flags, *[spectra] * 3)


def place_of(me, win):
    apart = jnp.bitwise_xor(me, win)
    return (apart & 48) + ((apart >> 1) & 3) * 4 + ((apart >> 3) & 1) * 2 + (apart & 1)


def spread_slots(real, imag, source, pick, held, src, win, bins):
    held[win] = dot(pick, jnp.concatenate([real, imag], axis=1))
    real = source[:SRC].astype(jnp.float32)
    imag = source[SRC:].astype(jnp.float32)
    for k, rows in enumerate((real, imag, real + imag)):
        for t in range(bins // 128):
            src[win, t, k * SRC : (k + 1) * SRC] = rows[:, t * 128 : (t + 1) * 128]


def correlate(held, src, total, sources, bins, steps):
    def group(i, _):
        rows = [pl.ds(pl.multiple_of(i * TALL + r, 8), 8) for r in range(0, TALL, 8)]
        for t in range(0, bins, 128):
            lanes = [slice(k * bins + t, k * bins + t + 128) for k in range(3)]
            for some in range(0, len(sources), SB):
                sums = [[[total[some + n, row, at] for row in rows] for at in lanes] for n in range(SB)]
                for win in range(steps):
                    real = [held[win, row, lanes[0]] for row in rows]
                    imag = [held[win, row, lanes[1]] for row in rows]
                    less = [x - y for x, y in zip(real, imag)]
                    for n in range(SB):
                        for k, values in enumerate((real, imag, less)):
                            a = src[win, t // 128, pl.ds(k * SRC + sources[some + n], 8, stride=0), :]
                            for r, b in enumerate(values):
                                sums[n][k][r] += a * b
                for n in range(SB):
                    for k, at in enumerate(lanes):
                        for r, row in enumerate(rows):
                            total[some + n, row, at] = sums[n][k][r]
        return 0

    lax.fori_loop(0, WIDE // TALL, group, 0)


def store_sums(total, n, out, q, bins):
    p, m, r = (total[n, :, k * bins : (k + 1) * bins] for k in range(3))
    out[q, :, :bins] = (p + m).astype(out.dtype)
    out[q, :, bins:] = (r - p + m).astype(out.dtype)


def first_kernel(me, got, source, theirs, mine, picks, count, held, src, total):
    step = pl.program_id(0)

    @pl.when(step == 0)
    def _():
        total[...] = jnp.zeros_like(total)
        count[...] = jnp.zeros_like(count)

    for win in range(STEP_A):
        notes = got[win, CAP:SLOTS, :].astype(jnp.float32)
        key = jnp.transpose(notes)[:WIDE, 0:1]
        pick = one_hot(iota((WIDE, SLOTS), 1) == key.astype(jnp.int32))
        picks[win] = pick
        count[...] += jnp.where(key > -0.5, 1.0, 0.0) * notes[1:2, :128]
        rows = source[place_of(me[0], step * STEP_A + win), :, :BINS_A]
        spread_slots(got[win, :CAP, :], got[win, SLOTS:, :], rows, pick[:, :CAP], held, src, win, BINS_A)
    correlate(held, src, total, range(SRC), BINS_A, STEP_A)

    @pl.when(step == pl.num_programs(0) - 1)
    def _():
        for q in range(SB):
            store_sums(total, q, theirs, q, BINS_A)
            store_sums(total, SB + q, mine, q, BINS_A)


def first_sums(me, got, source):
    shape = (SB, WIDE, 2 * BINS_A)
    sums_spec = pl.BlockSpec(shape, lambda g: (0, 0, 0))
    return pl.pallas_call(
        first_kernel,
        grid=(WINS // STEP_A,),
        in_specs=[
            pl.BlockSpec(memory_space=pltpu.SMEM),
            pl.BlockSpec((STEP_A, SLOTS + CAP, BINS_A), lambda g: (g, 0, 0)),
            pl.BlockSpec((WINS, 2 * SRC, F), lambda g: (0, 0, 0)),
        ],
        out_specs=[
            sums_spec,
            sums_spec,
            pl.BlockSpec((STEP_A, WIDE, SLOTS), lambda g: (g, 0, 0)),
            pl.BlockSpec((WIDE, 128), lambda g: (0, 0)),
        ],
        out_shape=[
            jax.ShapeDtypeStruct(shape, jnp.bfloat16),
            jax.ShapeDtypeStruct(shape, jnp.float32),
            jax.ShapeDtypeStruct((WINS, WIDE, SLOTS), jnp.bfloat16),
            jax.ShapeDtypeStruct((WIDE, 128), jnp.float32),
        ],
        scratch_shapes=[
            pltpu.VMEM((STEP_A, WIDE, 2 * BINS_A), jnp.float32),
            pltpu.VMEM((STEP_A, BINS_A // 128, 3 * SRC, 128), jnp.float32),
            pltpu.VMEM((SRC, WIDE, 3 * BINS_A), jnp.float32),
        ],
        cost_estimate=pl.CostEstimate(flops=30_000_000_000, bytes_accessed=20_000_000, transcendentals=0),
        compiler_params=pltpu.CompilerParams(vmem_limit_bytes=GRANT),
        name="cross_sums_first",
    )(me, got, source)


def second_kernel(first, me, got, source, picks, out, held, src, total):
    step = pl.program_id(0)

    @pl.when(step == 0)
    def _():
        total[...] = jnp.zeros_like(total)

    for win in range(STEP_B):
        rows = source[place_of(me[0], step * STEP_B + win), :, BINS_A:]
        spread_slots(got[win, :CAP, :], got[win, CAP:, :], rows, picks[win, :, :CAP], held, src, win, BINS_B)
    correlate(held, src, total, range(first, first + SB), BINS_B, STEP_B)

    @pl.when(step == pl.num_programs(0) - 1)
    def _():
        for q in range(SB):
            store_sums(total, q, out, q, BINS_B)


def second_sums(me, got, source, picks, first, dtype):
    shape = (SB, WIDE, 2 * BINS_B)
    return pl.pallas_call(
        functools.partial(second_kernel, first),
        grid=(WINS // STEP_B,),
        in_specs=[
            pl.BlockSpec(memory_space=pltpu.SMEM),
            pl.BlockSpec((STEP_B, 2 * CAP, BINS_B), lambda g: (g, 0, 0)),
            pl.BlockSpec((WINS, 2 * SRC, F), lambda g: (0, 0, 0)),
            pl.BlockSpec((STEP_B, WIDE, SLOTS), lambda g: (g, 0, 0)),
        ],
        out_specs=pl.BlockSpec(shape, lambda g: (0, 0, 0)),
        out_shape=jax.ShapeDtypeStruct(shape, dtype),
        scratch_shapes=[
            pltpu.VMEM((STEP_B, WIDE, 2 * BINS_B), jnp.float32),
            pltpu.VMEM((STEP_B, BINS_B // 128, 3 * SRC, 128), jnp.float32),
            pltpu.VMEM((SB, WIDE, 3 * BINS_B), jnp.float32),
        ],
        cost_estimate=pl.CostEstimate(flops=8_000_000_000, bytes_accessed=8_000_000, transcendentals=0),
        compiler_params=pltpu.CompilerParams(vmem_limit_bytes=GRANT),
        name="cross_sums_second",
    )(me, got, source, picks)


def lags_kernel(mine_a, from_a, mine_b, from_b, table, count, count_from, out, held, scale):
    @pl.when(pl.program_id(0) == 0)
    def _():
        for mine, got, at in ((mine_a, from_a, slice(0, 2 * BINS_A)), (mine_b, from_b, slice(2 * BINS_A, 2 * F))):
            held[:, at] = (mine[...] + got[...].astype(jnp.float32)).astype(jnp.bfloat16)
        for q in range(SB):
            pairs = count[:, SB + q : SB + q + 1] + count_from[:, q : q + 1]
            scale[q * WIDE : (q + 1) * WIDE] = jnp.broadcast_to(1.0 / jnp.maximum(pairs, 1.0), (WIDE, 128))

    out[...] = dot(held[...], table[...]) * scale[:, 0:1]


def to_lags(mine_a, from_a, mine_b, from_b, table, count, count_from):
    rows = SB * WIDE
    full = lambda shape: pl.BlockSpec(shape, lambda n: (0, 0))
    sums = [full((rows, 2 * bins)) for bins in (BINS_A, BINS_A, BINS_B, BINS_B)]
    tiled = pl.BlockSpec((2 * F, LAG_TILE), lambda n: (0, n))
    return pl.pallas_call(
        lags_kernel,
        grid=(pl.cdiv(LAGS, LAG_TILE),),
        in_specs=[*sums, tiled, full((WIDE, 128)), full((WIDE, 128))],
        out_specs=pl.BlockSpec((rows, LAG_TILE), lambda n: (0, n)),
        out_shape=jax.ShapeDtypeStruct((rows, LAGS), jnp.float32),
        scratch_shapes=[
            pltpu.VMEM((rows, 2 * F), jnp.bfloat16),
            pltpu.VMEM((rows, 128), jnp.float32),
        ],
        cost_estimate=pl.CostEstimate(flops=4 * rows * F * LAGS, bytes_accessed=4 * rows * LAGS * 2, transcendentals=0),
        compiler_params=pltpu.CompilerParams(vmem_limit_bytes=LAG_GRANT),
        name="to_lags",
    )(*(x.reshape(rows, -1) for x in (mine_a, from_a, mine_b, from_b)), table, count, count_from)


def lag_table(zero):
    row = jnp.arange(2 * F, dtype=jnp.int32) + zero
    last = row >= 2 * BINS_A
    bins = jnp.where(last, BINS_B, BINS_A)
    inside = jnp.where(last, row - 2 * BINS_A, row)
    bin_index = F0 + jnp.where(last, BINS_A, 0) + inside % bins
    lag_index = jnp.arange(LAGS, dtype=jnp.int32) - MAXLAG
    phase_steps = jnp.mod(bin_index[:, None] * lag_index[None, :], NFFT)
    angles = phase_steps.astype(jnp.float32) * jnp.float32(2.0 * math.pi / NFFT)
    table = jnp.where((inside < bins)[:, None], jnp.cos(angles), -jnp.sin(angles))
    return table.astype(jnp.bfloat16)


def swap(x):
    return lax.ppermute(x, "tm", [(0, 1), (1, 0)])


def gather_sources(rows):
    def partner(i, bits, r):
        for n, bit in enumerate(bits):
            i ^= ((r >> n) & 1) << bit
        return i

    for bits in ((0, 3), (1, 2), (4, 5)):
        steps = [[(i, partner(i, bits, r)) for i in range(BLOCKS)] for r in range(1, 4)]
        rows = jnp.concatenate([rows, *[lax.ppermute(rows, "chan", step) for step in steps]], axis=0)
    return rows


def local(spectra, mask):
    me = lax.axis_index("chan").astype(jnp.int32)[None]
    tm_index = lax.axis_index("tm").astype(jnp.int32)[None]
    mask = mask.reshape(LINES, 128)
    spectra = spectra.reshape(CH, 2, F)
    source, flags = source_rows(tm_index, mask, spectra)
    send_a, send_b = pack(mask, flags, spectra)
    send_a, source, zero = lax.optimization_barrier((send_a, source, jnp.int32(0)))
    table = lag_table(zero)
    source = gather_sources(source)
    send_b, table, source = lax.optimization_barrier((send_b, table, source))
    exchange = lambda x: lax.all_to_all(x, "chan", split_axis=0, concat_axis=0, tiled=True)
    got_a = exchange(send_a)
    got_b = exchange(send_b)
    theirs_a, mine_a, picks, count = first_sums(me, got_a, source)
    from_a = swap(theirs_a)
    count_from = swap(count)
    theirs_b = second_sums(me, got_b, source, picks, 0, jnp.bfloat16)
    from_b = swap(theirs_b)
    mine_b = second_sums(me, got_b, source, picks, SB, jnp.float32)
    lagged = to_lags(mine_a, from_a, mine_b, from_b, table, count, count_from)
    return lagged.reshape(SB, WIDE, LAGS)


def solution(mesh):
    placed = (P("tm", "chan", None, None, None), P("tm", "chan", None))
    return jax.shard_map(
        local, mesh=mesh, in_specs=placed, out_specs=P("tm", "chan", None), check_vma=False
    )
```

```python
import functools
import math

import jax
import jax.numpy as jnp
from jax import lax
from jax.experimental import pallas as pl
from jax.experimental.pallas import tpu as pltpu
from jax.sharding import PartitionSpec as P

CH = 10240
F = 384
F0 = 12
NFFT = 6000
MAXLAG = 1500
SB = 4
SRC = 8
LAGS = 3001
BLOCKS = 64
WIDE = 160
WINS = 64
LINES = 80
SLOTS = 128
ROWS = 2 * SLOTS
BINS_A = 256
BINS_B = 128
CAP = 120
PACK = 8
GRANT = 56 << 20
LAG_GRANT = 44 << 20
STEP_A = 16
STEP_B = 16
TALL = 32
LAG_TILE = 1024


def iota(shape, dim):
    return lax.broadcasted_iota(jnp.int32, shape, dim)


def one_hot(where):
    return jnp.where(where, 1.0, 0.0).astype(jnp.bfloat16)


def dot(a, b):
    return jnp.dot(a, b, preferred_element_type=jnp.float32)


def source_kernel(tm_ref, mask_ref, a0, a1, a2, b0, b1, b2, out, flag_out):
    middle = LINES // 2
    shift = SB * (1 - tm_ref[0])
    ones = lambda at: jnp.broadcast_to(mask_ref[at : at + 1, :], (16, 128)).astype(jnp.float32).astype(jnp.bfloat16)
    flags_a, flags_b = ones(0), ones(middle)
    lane = iota((128, 128), 1)
    row = iota((128, 128), 0)
    source = (lane + shift) % SRC
    here = (row == source % SB) & (lane < SRC)
    flag_out[...] = (dot(flags_a, one_hot(here & (source < SB))) + dot(flags_b, one_hot(here & (source >= SB))))[:8]
    twice = one_hot(row == lane // 2)
    kept_a, kept_b = dot(flags_a, twice), dot(flags_b, twice)
    take = iota((2 * SRC, 16), 0)
    lane = iota((2 * SRC, 16), 1)
    source = (take % SRC + shift) % SRC
    hit = lane == 2 * (source % SB) + take // SRC
    pick_a = one_hot(hit & (source < SB) & (kept_a[:, :16] > 0.5))
    pick_b = one_hot(hit & (source >= SB) & (kept_b[:, :16] > 0.5))
    rows = [
        dot(pick_a, ra.reshape(16, 128)[...]) + dot(pick_b, rb.reshape(16, 128)[...])
        for ra, rb in ((a0, b0), (a1, b1), (a2, b2))
    ]
    squares = sum(r * r for r in rows)
    energy = jnp.sum(squares[:SRC] + squares[SRC:], axis=1, keepdims=True) / F
    factor = lax.rsqrt(energy + 1e-06)
    factor = jnp.concatenate([factor, factor], axis=0)
    for k, r in enumerate(rows):
        out[0, :, k * 128 : (k + 1) * 128] = (r * factor).astype(jnp.bfloat16)


def source_rows(tm_index, mask, spectra):
    head = lambda k, at: pl.BlockSpec((8, 2, 128), lambda i: (at, 0, k))
    middle = BLOCKS // 2 * WIDE // 8
    return pl.pallas_call(
        source_kernel,
        grid=(1,),
        in_specs=[
            pl.BlockSpec(memory_space=pltpu.SMEM),
            pl.BlockSpec((LINES, 128), lambda i: (0, 0)),
            *[head(k, 0) for k in range(3)],
            *[head(k, middle) for k in range(3)],
        ],
        out_specs=[
            pl.BlockSpec((1, 2 * SRC, F), lambda i: (0, 0, 0)),
            pl.BlockSpec((8, 128), lambda i: (0, 0)),
        ],
        out_shape=[
            jax.ShapeDtypeStruct((1, 2 * SRC, F), jnp.bfloat16),
            jax.ShapeDtypeStruct((8, 128), jnp.float32),
        ],
        cost_estimate=pl.CostEstimate(flops=10_000_000, bytes_accessed=100_000, transcendentals=0),
        name="source_rows",
    )(tm_index, mask, *[spectra] * 6)


def pack_kernel(mask_ref, src_ref, flag_ref, x0, x1, x2, send_a, send_b, slot_ref, key_ref):
    step = pl.program_id(0)

    @pl.when(step == 0)
    def _():
        lines = [mask_ref[pl.ds(k, LINES // 5, stride=5), :] for k in range(5)]
        lines = jnp.concatenate(lines, axis=1).astype(jnp.float32)
        lane = iota((WIDE, 2 * WIDE), 1)
        row = iota((WIDE, 2 * WIDE), 0)
        ahead_two, here_two = one_hot(row < lane // 2), one_hot(row == lane // 2)
        part = (iota((LINES // 5, 2 * WIDE), 1) % 2).astype(jnp.float32)
        lane = iota((WIDE, BINS_A), 1)
        row = iota((WIDE, BINS_A), 0)
        ahead, here = one_hot(row < lane), one_hot(row == lane)
        for m in range(4):
            flags = lines[:, m * WIDE : (m + 1) * WIDE].astype(jnp.bfloat16)
            slot_ref[m] = jnp.where(dot(flags, here_two) > 0.5, dot(flags, ahead_two) + part * SLOTS, -1.0)
            key_ref[m] = jnp.where(dot(flags, here) > 0.5, dot(flags, ahead), -1.0)

    flag_line = flag_ref[:1, :]
    flag_line = jnp.concatenate([flag_line, flag_line], axis=1)
    place = iota((ROWS, 2 * WIDE), 0).astype(jnp.float32).astype(jnp.bfloat16)
    for n in range(PACK):
        four = pl.ds(step * (PACK // 4) + n // 4, 1)
        slot = slot_ref[n % 4, four, :].astype(jnp.bfloat16)
        pick = jnp.where(place == slot, jnp.ones_like(place), jnp.zeros_like(place))
        at = pl.ds(n * 2 * WIDE, 2 * WIDE)
        band = jnp.concatenate([r.reshape(PACK * 2 * WIDE, 128)[at, :] for r in (x0, x1, x2)], axis=1)
        rows = dot(pick, band)
        real, imag = rows[:CAP], rows[SLOTS : SLOTS + CAP]
        energy = jnp.sum(real * real + imag * imag, axis=1, keepdims=True) / F
        factor = lax.rsqrt(energy + 1e-06)
        real = (real * factor).astype(jnp.bfloat16)
        imag = (imag * factor).astype(jnp.bfloat16)
        for out, lo, hi in ((send_a, 0, BINS_A), (send_b, BINS_A, F)):
            out[n, :CAP] = real[:, lo:hi]
            out[n, CAP:SLOTS] = src_ref[0, :SRC, lo:hi]
            out[n, SLOTS : SLOTS + CAP] = imag[:, lo:hi]
            out[n, SLOTS + CAP : ROWS] = src_ref[0, SRC:, lo:hi]
        line = iota((8, BINS_A), 0)
        notes = jnp.where(line == 0, key_ref[n % 4, four, :], flag_line)
        send_a[n, ROWS:] = notes.astype(jnp.bfloat16)


def pack(mask, source, flags, spectra):
    band = lambda k: pl.BlockSpec((PACK * WIDE, 2, 128), lambda b: (b, 0, k))
    return pl.pallas_call(
        pack_kernel,
        grid=(BLOCKS // PACK,),
        in_specs=[
            pl.BlockSpec((LINES, 128), lambda b: (0, 0)),
            pl.BlockSpec((1, 2 * SRC, F), lambda b: (0, 0, 0)),
            pl.BlockSpec((8, 128), lambda b: (0, 0)),
            *[band(k) for k in range(3)],
        ],
        out_specs=[
            pl.BlockSpec((PACK, ROWS + 8, BINS_A), lambda b: (b, 0, 0)),
            pl.BlockSpec((PACK, ROWS, BINS_B), lambda b: (b, 0, 0)),
        ],
        out_shape=[
            jax.ShapeDtypeStruct((BLOCKS, ROWS + 8, BINS_A), jnp.bfloat16),
            jax.ShapeDtypeStruct((BLOCKS, ROWS, BINS_B), jnp.bfloat16),
        ],
        scratch_shapes=[
            pltpu.VMEM((4, BLOCKS // 4, 2 * WIDE), jnp.float32),
            pltpu.VMEM((4, BLOCKS // 4, BINS_A), jnp.float32),
        ],
        cost_estimate=pl.CostEstimate(flops=2 * BLOCKS * ROWS * 2 * WIDE * F, bytes_accessed=30_000_000, transcendentals=0),
        compiler_params=pltpu.CompilerParams(vmem_limit_bytes=GRANT),
        name="whiten_pack",
    )(mask, source, flags, *[spectra] * 3)


def spread_slots(got, pick, held, src, win, bins):
    rows = jnp.concatenate([got[win, :SLOTS, :], got[win, SLOTS:ROWS, :]], axis=1)
    held[win] = dot(pick, rows)
    real = rows[CAP:, :bins].astype(jnp.float32)
    imag = rows[CAP:, bins:].astype(jnp.float32)
    for k, rows in enumerate((real, imag, real + imag)):
        for t in range(bins // 128):
            src[win, t, k * SRC : (k + 1) * SRC] = rows[:, t * 128 : (t + 1) * 128]


def correlate(held, src, total, sources, bins, steps):
    def group(i, _):
        rows = [pl.ds(pl.multiple_of(i * TALL + r, 8), 8) for r in range(0, TALL, 8)]
        for t in range(0, bins, 128):
            lanes = [slice(k * bins + t, k * bins + t + 128) for k in range(3)]
            for some in range(0, len(sources), SB):
                sums = [[[total[some + n, row, at] for row in rows] for at in lanes] for n in range(SB)]
                for win in range(steps):
                    real = [held[win, row, lanes[0]] for row in rows]
                    imag = [held[win, row, lanes[1]] for row in rows]
                    less = [x - y for x, y in zip(real, imag)]
                    for n in range(SB):
                        for k, values in enumerate((real, imag, less)):
                            a = src[win, t // 128, pl.ds(k * SRC + sources[some + n], 8, stride=0), :]
                            for r, b in enumerate(values):
                                sums[n][k][r] += a * b
                for n in range(SB):
                    for k, at in enumerate(lanes):
                        for r, row in enumerate(rows):
                            total[some + n, row, at] = sums[n][k][r]
        return 0

    lax.fori_loop(0, WIDE // TALL, group, 0)


def store_sums(total, n, out, q, bins):
    p, m, r = (total[n, :, k * bins : (k + 1) * bins] for k in range(3))
    out[q, :, :bins] = (p + m).astype(out.dtype)
    out[q, :, bins:] = (r - p + m).astype(out.dtype)


def first_kernel(got, theirs, mine, picks, count, held, src, total):
    step = pl.program_id(0)

    @pl.when(step == 0)
    def _():
        total[...] = jnp.zeros_like(total)
        count[...] = jnp.zeros_like(count)

    for win in range(STEP_A):
        notes = got[win, ROWS:, :].astype(jnp.float32)
        key = jnp.transpose(notes)[:WIDE, 0:1]
        pick = one_hot(iota((WIDE, SLOTS), 1) == key.astype(jnp.int32))
        picks[win] = pick
        count[...] += jnp.where(key > -0.5, 1.0, 0.0) * notes[1:2, :128]
        spread_slots(got, pick, held, src, win, BINS_A)
    correlate(held, src, total, range(SRC), BINS_A, STEP_A)

    @pl.when(step == pl.num_programs(0) - 1)
    def _():
        for q in range(SB):
            store_sums(total, q, theirs, q, BINS_A)
            store_sums(total, SB + q, mine, q, BINS_A)


def first_sums(got):
    shape = (SB, WIDE, 2 * BINS_A)
    sums_spec = pl.BlockSpec(shape, lambda g: (0, 0, 0))
    return pl.pallas_call(
        first_kernel,
        grid=(WINS // STEP_A,),
        in_specs=[pl.BlockSpec((STEP_A, ROWS + 8, BINS_A), lambda g: (g, 0, 0))],
        out_specs=[
            sums_spec,
            sums_spec,
            pl.BlockSpec((STEP_A, WIDE, SLOTS), lambda g: (g, 0, 0)),
            pl.BlockSpec((WIDE, 128), lambda g: (0, 0)),
        ],
        out_shape=[
            jax.ShapeDtypeStruct(shape, jnp.bfloat16),
            jax.ShapeDtypeStruct(shape, jnp.float32),
            jax.ShapeDtypeStruct((WINS, WIDE, SLOTS), jnp.bfloat16),
            jax.ShapeDtypeStruct((WIDE, 128), jnp.float32),
        ],
        scratch_shapes=[
            pltpu.VMEM((STEP_A, WIDE, 2 * BINS_A), jnp.float32),
            pltpu.VMEM((STEP_A, BINS_A // 128, 3 * SRC, 128), jnp.float32),
            pltpu.VMEM((SRC, WIDE, 3 * BINS_A), jnp.float32),
        ],
        cost_estimate=pl.CostEstimate(flops=30_000_000_000, bytes_accessed=20_000_000, transcendentals=0),
        compiler_params=pltpu.CompilerParams(vmem_limit_bytes=GRANT),
        name="cross_sums_first",
    )(got)


def second_kernel(first, got, picks, out, held, src, total):
    step = pl.program_id(0)

    @pl.when(step == 0)
    def _():
        total[...] = jnp.zeros_like(total)

    for win in range(STEP_B):
        spread_slots(got, picks[win], held, src, win, BINS_B)
    correlate(held, src, total, range(first, first + SB), BINS_B, STEP_B)

    @pl.when(step == pl.num_programs(0) - 1)
    def _():
        for q in range(SB):
            store_sums(total, q, out, q, BINS_B)


def second_sums(got, picks, first, dtype, grant):
    shape = (SB, WIDE, 2 * BINS_B)
    return pl.pallas_call(
        functools.partial(second_kernel, first),
        grid=(WINS // STEP_B,),
        in_specs=[
            pl.BlockSpec((STEP_B, ROWS, BINS_B), lambda g: (g, 0, 0)),
            pl.BlockSpec((STEP_B, WIDE, SLOTS), lambda g: (g, 0, 0)),
        ],
        out_specs=pl.BlockSpec(shape, lambda g: (0, 0, 0)),
        out_shape=jax.ShapeDtypeStruct(shape, dtype),
        scratch_shapes=[
            pltpu.VMEM((STEP_B, WIDE, 2 * BINS_B), jnp.float32),
            pltpu.VMEM((STEP_B, BINS_B // 128, 3 * SRC, 128), jnp.float32),
            pltpu.VMEM((SB, WIDE, 3 * BINS_B), jnp.float32),
        ],
        cost_estimate=pl.CostEstimate(flops=8_000_000_000, bytes_accessed=8_000_000, transcendentals=0),
        compiler_params=pltpu.CompilerParams(vmem_limit_bytes=grant),
        name="cross_sums_second",
    )(got, picks)


def lags_kernel(mine_a, from_a, mine_b, from_b, table, count, count_from, out, held, scale):
    @pl.when(pl.program_id(0) == 0)
    def _():
        for mine, got, at in ((mine_a, from_a, slice(0, 2 * BINS_A)), (mine_b, from_b, slice(2 * BINS_A, 2 * F))):
            held[:, at] = (mine[...] + got[...].astype(jnp.float32)).astype(jnp.bfloat16)
        for q in range(SB):
            pairs = count[:, SB + q : SB + q + 1] + count_from[:, q : q + 1]
            scale[q * WIDE : (q + 1) * WIDE] = jnp.broadcast_to(1.0 / jnp.maximum(pairs, 1.0), (WIDE, 128))

    out[...] = dot(held[...], table[...]) * scale[:, 0:1]


def to_lags(mine_a, from_a, mine_b, from_b, table, count, count_from):
    rows = SB * WIDE
    full = lambda shape: pl.BlockSpec(shape, lambda n: (0, 0))
    sums = [full((rows, 2 * bins)) for bins in (BINS_A, BINS_A, BINS_B, BINS_B)]
    tiled = pl.BlockSpec((2 * F, LAG_TILE), lambda n: (0, n))
    return pl.pallas_call(
        lags_kernel,
        grid=(pl.cdiv(LAGS, LAG_TILE),),
        in_specs=[*sums, tiled, full((WIDE, 128)), full((WIDE, 128))],
        out_specs=pl.BlockSpec((rows, LAG_TILE), lambda n: (0, n)),
        out_shape=jax.ShapeDtypeStruct((rows, LAGS), jnp.float32),
        scratch_shapes=[
            pltpu.VMEM((rows, 2 * F), jnp.bfloat16),
            pltpu.VMEM((rows, 128), jnp.float32),
        ],
        cost_estimate=pl.CostEstimate(flops=4 * rows * F * LAGS, bytes_accessed=4 * rows * LAGS * 2, transcendentals=0),
        compiler_params=pltpu.CompilerParams(vmem_limit_bytes=LAG_GRANT),
        name="to_lags",
    )(*(x.reshape(rows, -1) for x in (mine_a, from_a, mine_b, from_b)), table, count, count_from)


def lag_table(zero):
    row = jnp.arange(2 * F, dtype=jnp.int32) + zero
    last = row >= 2 * BINS_A
    bins = jnp.where(last, BINS_B, BINS_A)
    inside = jnp.where(last, row - 2 * BINS_A, row)
    bin_index = F0 + jnp.where(last, BINS_A, 0) + inside % bins
    lag_index = jnp.arange(LAGS, dtype=jnp.int32) - MAXLAG
    phase_steps = jnp.mod(bin_index[:, None] * lag_index[None, :], NFFT)
    angles = phase_steps.astype(jnp.float32) * jnp.float32(2.0 * math.pi / NFFT)
    table = jnp.where((inside < bins)[:, None], jnp.cos(angles), -jnp.sin(angles))
    return table.astype(jnp.bfloat16)


def swap(x):
    return lax.ppermute(x, "tm", [(0, 1), (1, 0)])


def local(spectra, mask):
    tm_index = lax.axis_index("tm").astype(jnp.int32)[None]
    mask = mask.reshape(LINES, 128)
    spectra = spectra.reshape(CH, 2, F)
    source, flags = source_rows(tm_index, mask, spectra)
    send_a, send_b = pack(mask, source, flags, spectra)
    send_a, zero = lax.optimization_barrier((send_a, jnp.int32(0)))
    table = lag_table(zero)
    send_b, table = lax.optimization_barrier((send_b, table))
    exchange = lambda x: lax.all_to_all(x, "chan", split_axis=0, concat_axis=0, tiled=True)
    got_a = exchange(send_a)
    got_b = exchange(send_b)
    theirs_a, mine_a, picks, count = first_sums(got_a)
    from_a = swap(theirs_a)
    count_from = swap(count)
    got_b, count_from = lax.optimization_barrier((got_b, count_from))
    theirs_b = second_sums(got_b, picks, 0, jnp.bfloat16, GRANT)
    from_b = swap(theirs_b)
    mine_b = second_sums(got_b, picks, SB, jnp.float32, GRANT // 2)
    lagged = to_lags(mine_a, from_a, mine_b, from_b, table, count, count_from)
    return lagged.reshape(SB, WIDE, LAGS)


def solution(mesh):
    placed = (P("tm", "chan", None, None, None), P("tm", "chan", None))
    return jax.shard_map(
        local, mesh=mesh, in_specs=placed, out_specs=P("tm", "chan", None), check_vma=False
    )
```

```python
import functools
import math

import jax
import jax.numpy as jnp
from jax import lax
from jax.experimental import pallas as pl
from jax.experimental.pallas import tpu as pltpu
from jax.sharding import PartitionSpec as P

CH = 10240
F = 384
F0 = 12
NFFT = 6000
MAXLAG = 1500
SB = 4
SRC = 8
LAGS = 3001
BLOCKS = 64
WIDE = 160
WINS = 64
LINES = 80
SLOTS = 128
ROWS = 2 * SLOTS
BINS_A = 256
BINS_B = 128
CAP = 120
PACK = 8
GRANT = 56 << 20
LAG_GRANT = 44 << 20
STEP_A = 16
STEP_B = 16
TALL = 32
LAG_TILE = 1024


def iota(shape, dim):
    return lax.broadcasted_iota(jnp.int32, shape, dim)


def one_hot(where):
    return jnp.where(where, 1.0, 0.0).astype(jnp.bfloat16)


def dot(a, b):
    return jnp.dot(a, b, preferred_element_type=jnp.float32)


def source_kernel(tm_ref, mask_ref, a0, a1, a2, b0, b1, b2, out, flag_out):
    middle = LINES // 2
    shift = SB * (1 - tm_ref[0])
    ones = lambda at: jnp.broadcast_to(mask_ref[at : at + 1, :], (16, 128)).astype(jnp.float32).astype(jnp.bfloat16)
    flags_a, flags_b = ones(0), ones(middle)
    lane = iota((128, 128), 1)
    row = iota((128, 128), 0)
    source = (lane + shift) % SRC
    here = (row == source % SB) & (lane < SRC)
    flag_out[...] = (dot(flags_a, one_hot(here & (source < SB))) + dot(flags_b, one_hot(here & (source >= SB))))[:8]
    twice = one_hot(row == lane // 2)
    kept_a, kept_b = dot(flags_a, twice), dot(flags_b, twice)
    take = iota((2 * SRC, 16), 0)
    lane = iota((2 * SRC, 16), 1)
    source = (take % SRC + shift) % SRC
    hit = lane == 2 * (source % SB) + take // SRC
    pick_a = one_hot(hit & (source < SB) & (kept_a[:, :16] > 0.5))
    pick_b = one_hot(hit & (source >= SB) & (kept_b[:, :16] > 0.5))
    rows = [
        dot(pick_a, ra.reshape(16, 128)[...]) + dot(pick_b, rb.reshape(16, 128)[...])
        for ra, rb in ((a0, b0), (a1, b1), (a2, b2))
    ]
    squares = sum(r * r for r in rows)
    energy = jnp.sum(squares[:SRC] + squares[SRC:], axis=1, keepdims=True) / F
    factor = lax.rsqrt(energy + 1e-06)
    factor = jnp.concatenate([factor, factor], axis=0)
    for k, r in enumerate(rows):
        out[0, :, k * 128 : (k + 1) * 128] = (r * factor).astype(jnp.bfloat16)


def pack_kernel(tm_ref, mask_ref, *refs):
    heads, (x0, x1, x2, send_a, send_b, slot_ref, key_ref, src_ref, flag_ref) = refs[:6], refs[6:]
    step = pl.program_id(0)

    @pl.when(step == 0)
    def _():
        source_kernel(tm_ref, mask_ref, *heads, src_ref, flag_ref)
        lines = [mask_ref[pl.ds(k, LINES // 5, stride=5), :] for k in range(5)]
        lines = jnp.concatenate(lines, axis=1).astype(jnp.float32)
        lane = iota((WIDE, 2 * WIDE), 1)
        row = iota((WIDE, 2 * WIDE), 0)
        ahead_two, here_two = one_hot(row < lane // 2), one_hot(row == lane // 2)
        part = (iota((LINES // 5, 2 * WIDE), 1) % 2).astype(jnp.float32)
        lane = iota((WIDE, BINS_A), 1)
        row = iota((WIDE, BINS_A), 0)
        ahead, here = one_hot(row < lane), one_hot(row == lane)
        for m in range(4):
            flags = lines[:, m * WIDE : (m + 1) * WIDE].astype(jnp.bfloat16)
            slot_ref[m] = jnp.where(dot(flags, here_two) > 0.5, dot(flags, ahead_two) + part * CAP, -1.0)
            key_ref[m] = jnp.where(dot(flags, here) > 0.5, dot(flags, ahead), -1.0)

    flag_line = flag_ref[:1, :]
    flag_line = jnp.concatenate([flag_line, flag_line], axis=1)
    place = iota((2 * CAP, 2 * WIDE), 0).astype(jnp.float32).astype(jnp.bfloat16)
    for n in range(PACK):
        four = pl.ds(step * (PACK // 4) + n // 4, 1)
        slot = slot_ref[n % 4, four, :].astype(jnp.bfloat16)
        pick = jnp.where(place == slot, jnp.ones_like(place), jnp.zeros_like(place))
        at = pl.ds(n * 2 * WIDE, 2 * WIDE)
        band = jnp.concatenate([r.reshape(PACK * 2 * WIDE, 128)[at, :] for r in (x0, x1, x2)], axis=1)
        rows = dot(pick, band)
        real, imag = rows[:CAP], rows[CAP:]
        energy = jnp.sum(real * real + imag * imag, axis=1, keepdims=True) / F
        factor = lax.rsqrt(energy + 1e-06)
        real = (real * factor).astype(jnp.bfloat16)
        imag = (imag * factor).astype(jnp.bfloat16)
        for out, lo, hi in ((send_a, 0, BINS_A), (send_b, BINS_A, F)):
            out[n, :CAP] = real[:, lo:hi]
            out[n, CAP:SLOTS] = src_ref[0, :SRC, lo:hi]
            out[n, SLOTS : SLOTS + CAP] = imag[:, lo:hi]
            out[n, SLOTS + CAP : ROWS] = src_ref[0, SRC:, lo:hi]
        line = iota((8, BINS_A), 0)
        notes = jnp.where(line == 0, key_ref[n % 4, four, :], flag_line)
        send_a[n, ROWS:] = notes.astype(jnp.bfloat16)


def pack(tm_index, mask, spectra):
    head = lambda k, at: pl.BlockSpec((8, 2, 128), lambda b: (at, 0, k))
    middle = BLOCKS // 2 * WIDE // 8
    band = lambda k: pl.BlockSpec((PACK * WIDE, 2, 128), lambda b: (b, 0, k))
    return pl.pallas_call(
        pack_kernel,
        grid=(BLOCKS // PACK,),
        in_specs=[
            pl.BlockSpec(memory_space=pltpu.SMEM),
            pl.BlockSpec((LINES, 128), lambda b: (0, 0)),
            *[head(k, 0) for k in range(3)],
            *[head(k, middle) for k in range(3)],
            *[band(k) for k in range(3)],
        ],
        out_specs=[
            pl.BlockSpec((PACK, ROWS + 8, BINS_A), lambda b: (b, 0, 0)),
            pl.BlockSpec((PACK, ROWS, BINS_B), lambda b: (b, 0, 0)),
        ],
        out_shape=[
            jax.ShapeDtypeStruct((BLOCKS, ROWS + 8, BINS_A), jnp.bfloat16),
            jax.ShapeDtypeStruct((BLOCKS, ROWS, BINS_B), jnp.bfloat16),
        ],
        scratch_shapes=[
            pltpu.VMEM((4, BLOCKS // 4, 2 * WIDE), jnp.float32),
            pltpu.VMEM((4, BLOCKS // 4, BINS_A), jnp.float32),
            pltpu.VMEM((1, 2 * SRC, F), jnp.bfloat16),
            pltpu.VMEM((8, 128), jnp.float32),
        ],
        cost_estimate=pl.CostEstimate(flops=2 * BLOCKS * ROWS * 2 * WIDE * F, bytes_accessed=30_000_000, transcendentals=0),
        compiler_params=pltpu.CompilerParams(vmem_limit_bytes=GRANT),
        name="whiten_pack",
    )(tm_index, mask, *[spectra] * 9)


def spread_slots(got, pick, held, src, win, bins):
    rows = jnp.concatenate([got[win, :SLOTS, :], got[win, SLOTS:ROWS, :]], axis=1)
    held[win] = dot(pick, rows)
    real = rows[CAP:, :bins].astype(jnp.float32)
    imag = rows[CAP:, bins:].astype(jnp.float32)
    for k, rows in enumerate((real, imag, real + imag)):
        for t in range(bins // 128):
            src[win, t, k * SRC : (k + 1) * SRC] = rows[:, t * 128 : (t + 1) * 128]


def correlate(held, src, total, sources, bins, steps):
    def group(i, _):
        rows = [pl.ds(pl.multiple_of(i * TALL + r, 8), 8) for r in range(0, TALL, 8)]
        for t in range(0, bins, 128):
            lanes = [slice(k * bins + t, k * bins + t + 128) for k in range(3)]
            for some in range(0, len(sources), SB):
                sums = [[[total[some + n, row, at] for row in rows] for at in lanes] for n in range(SB)]
                for win in range(steps):
                    real = [held[win, row, lanes[0]] for row in rows]
                    imag = [held[win, row, lanes[1]] for row in rows]
                    less = [x - y for x, y in zip(real, imag)]
                    for n in range(SB):
                        for k, values in enumerate((real, imag, less)):
                            a = src[win, t // 128, pl.ds(k * SRC + sources[some + n], 8, stride=0), :]
                            for r, b in enumerate(values):
                                sums[n][k][r] += a * b
                for n in range(SB):
                    for k, at in enumerate(lanes):
                        for r, row in enumerate(rows):
                            total[some + n, row, at] = sums[n][k][r]
        return 0

    lax.fori_loop(0, WIDE // TALL, group, 0)


def store_sums(total, n, out, q, bins):
    p, m, r = (total[n, :, k * bins : (k + 1) * bins] for k in range(3))
    out[q, :, :bins] = (p + m).astype(out.dtype)
    out[q, :, bins:] = (r - p + m).astype(out.dtype)


def first_kernel(got, theirs, mine, picks, count, held, src, total):
    step = pl.program_id(0)

    @pl.when(step == 0)
    def _():
        total[...] = jnp.zeros_like(total)
        count[...] = jnp.zeros_like(count)

    for win in range(STEP_A):
        notes = got[win, ROWS:, :].astype(jnp.float32)
        key = jnp.transpose(notes)[:WIDE, 0:1]
        pick = one_hot(iota((WIDE, SLOTS), 1) == key.astype(jnp.int32))
        picks[win] = pick
        count[...] += jnp.where(key > -0.5, 1.0, 0.0) * notes[1:2, :128]
        spread_slots(got, pick, held, src, win, BINS_A)
    correlate(held, src, total, range(SRC), BINS_A, STEP_A)

    @pl.when(step == pl.num_programs(0) - 1)
    def _():
        for q in range(SB):
            store_sums(total, q, theirs, q, BINS_A)
            store_sums(total, SB + q, mine, q, BINS_A)


def first_sums(got):
    shape = (SB, WIDE, 2 * BINS_A)
    sums_spec = pl.BlockSpec(shape, lambda g: (0, 0, 0))
    return pl.pallas_call(
        first_kernel,
        grid=(WINS // STEP_A,),
        in_specs=[pl.BlockSpec((STEP_A, ROWS + 8, BINS_A), lambda g: (g, 0, 0))],
        out_specs=[
            sums_spec,
            sums_spec,
            pl.BlockSpec((STEP_A, WIDE, SLOTS), lambda g: (g, 0, 0)),
            pl.BlockSpec((WIDE, 128), lambda g: (0, 0)),
        ],
        out_shape=[
            jax.ShapeDtypeStruct(shape, jnp.bfloat16),
            jax.ShapeDtypeStruct(shape, jnp.float32),
            jax.ShapeDtypeStruct((WINS, WIDE, SLOTS), jnp.bfloat16),
            jax.ShapeDtypeStruct((WIDE, 128), jnp.float32),
        ],
        scratch_shapes=[
            pltpu.VMEM((STEP_A, WIDE, 2 * BINS_A), jnp.float32),
            pltpu.VMEM((STEP_A, BINS_A // 128, 3 * SRC, 128), jnp.float32),
            pltpu.VMEM((SRC, WIDE, 3 * BINS_A), jnp.float32),
        ],
        cost_estimate=pl.CostEstimate(flops=30_000_000_000, bytes_accessed=20_000_000, transcendentals=0),
        compiler_params=pltpu.CompilerParams(vmem_limit_bytes=GRANT),
        name="cross_sums_first",
    )(got)


def second_kernel(first, got, picks, out, held, src, total):
    step = pl.program_id(0)

    @pl.when(step == 0)
    def _():
        total[...] = jnp.zeros_like(total)

    for win in range(STEP_B):
        spread_slots(got, picks[win], held, src, win, BINS_B)
    correlate(held, src, total, range(first, first + SB), BINS_B, STEP_B)

    @pl.when(step == pl.num_programs(0) - 1)
    def _():
        for q in range(SB):
            store_sums(total, q, out, q, BINS_B)


def second_sums(got, picks, first, dtype, grant):
    shape = (SB, WIDE, 2 * BINS_B)
    return pl.pallas_call(
        functools.partial(second_kernel, first),
        grid=(WINS // STEP_B,),
        in_specs=[
            pl.BlockSpec((STEP_B, ROWS, BINS_B), lambda g: (g, 0, 0)),
            pl.BlockSpec((STEP_B, WIDE, SLOTS), lambda g: (g, 0, 0)),
        ],
        out_specs=pl.BlockSpec(shape, lambda g: (0, 0, 0)),
        out_shape=jax.ShapeDtypeStruct(shape, dtype),
        scratch_shapes=[
            pltpu.VMEM((STEP_B, WIDE, 2 * BINS_B), jnp.float32),
            pltpu.VMEM((STEP_B, BINS_B // 128, 3 * SRC, 128), jnp.float32),
            pltpu.VMEM((SB, WIDE, 3 * BINS_B), jnp.float32),
        ],
        cost_estimate=pl.CostEstimate(flops=8_000_000_000, bytes_accessed=8_000_000, transcendentals=0),
        compiler_params=pltpu.CompilerParams(vmem_limit_bytes=grant),
        name="cross_sums_second",
    )(got, picks)


def lags_kernel(mine_a, from_a, mine_b, from_b, table, count, count_from, out, held, scale):
    @pl.when(pl.program_id(0) == 0)
    def _():
        for mine, got, at in ((mine_a, from_a, slice(0, 2 * BINS_A)), (mine_b, from_b, slice(2 * BINS_A, 2 * F))):
            held[:, at] = (mine[...] + got[...].astype(jnp.float32)).astype(jnp.bfloat16)
        for q in range(SB):
            pairs = count[:, SB + q : SB + q + 1] + count_from[:, q : q + 1]
            scale[q * WIDE : (q + 1) * WIDE] = jnp.broadcast_to(1.0 / jnp.maximum(pairs, 1.0), (WIDE, 128))

    out[...] = dot(held[...], table[...]) * scale[:, 0:1]


def to_lags(mine_a, from_a, mine_b, from_b, table, count, count_from):
    rows = SB * WIDE
    full = lambda shape: pl.BlockSpec(shape, lambda n: (0, 0))
    sums = [full((rows, 2 * bins)) for bins in (BINS_A, BINS_A, BINS_B, BINS_B)]
    tiled = pl.BlockSpec((2 * F, LAG_TILE), lambda n: (0, n))
    return pl.pallas_call(
        lags_kernel,
        grid=(pl.cdiv(LAGS, LAG_TILE),),
        in_specs=[*sums, tiled, full((WIDE, 128)), full((WIDE, 128))],
        out_specs=pl.BlockSpec((rows, LAG_TILE), lambda n: (0, n)),
        out_shape=jax.ShapeDtypeStruct((rows, LAGS), jnp.float32),
        scratch_shapes=[
            pltpu.VMEM((rows, 2 * F), jnp.bfloat16),
            pltpu.VMEM((rows, 128), jnp.float32),
        ],
        cost_estimate=pl.CostEstimate(flops=4 * rows * F * LAGS, bytes_accessed=4 * rows * LAGS * 2, transcendentals=0),
        compiler_params=pltpu.CompilerParams(vmem_limit_bytes=LAG_GRANT),
        name="to_lags",
    )(*(x.reshape(rows, -1) for x in (mine_a, from_a, mine_b, from_b)), table, count, count_from)


def lag_table(zero):
    row = jnp.arange(2 * F, dtype=jnp.int32) + zero
    last = row >= 2 * BINS_A
    bins = jnp.where(last, BINS_B, BINS_A)
    inside = jnp.where(last, row - 2 * BINS_A, row)
    bin_index = F0 + jnp.where(last, BINS_A, 0) + inside % bins
    lag_index = jnp.arange(LAGS, dtype=jnp.int32) - MAXLAG
    phase_steps = jnp.mod(bin_index[:, None] * lag_index[None, :], NFFT)
    angles = phase_steps.astype(jnp.float32) * jnp.float32(2.0 * math.pi / NFFT)
    table = jnp.where((inside < bins)[:, None], jnp.cos(angles), -jnp.sin(angles))
    return table.astype(jnp.bfloat16)


def swap(x):
    return lax.ppermute(x, "tm", [(0, 1), (1, 0)])


def local(spectra, mask):
    tm_index = lax.axis_index("tm").astype(jnp.int32)[None]
    mask = mask.reshape(LINES, 128)
    spectra = spectra.reshape(CH, 2, F)
    send_a, send_b = pack(tm_index, mask, spectra)
    send_a, zero = lax.optimization_barrier((send_a, jnp.int32(0)))
    table = lag_table(zero)
    send_b, table = lax.optimization_barrier((send_b, table))
    exchange = lambda x: lax.all_to_all(x, "chan", split_axis=0, concat_axis=0, tiled=True)
    got_a = exchange(send_a)
    got_b = exchange(send_b)
    theirs_a, mine_a, picks, count = first_sums(got_a)
    from_a = swap(theirs_a)
    count_from = swap(count)
    got_b, count_from = lax.optimization_barrier((got_b, count_from))
    theirs_b = second_sums(got_b, picks, 0, jnp.bfloat16, GRANT)
    from_b = swap(theirs_b)
    mine_b = second_sums(got_b, picks, SB, jnp.float32, GRANT // 2)
    lagged = to_lags(mine_a, from_a, mine_b, from_b, table, count, count_from)
    return lagged.reshape(SB, WIDE, LAGS)


def solution(mesh):
    placed = (P("tm", "chan", None, None, None), P("tm", "chan", None))
    return jax.shard_map(
        local, mesh=mesh, in_specs=placed, out_specs=P("tm", "chan", None), check_vma=False
    )
```

```python
import functools
import math

import jax
import jax.numpy as jnp
from jax import lax
from jax.experimental import pallas as pl
from jax.experimental.pallas import tpu as pltpu
from jax.sharding import PartitionSpec as P

CH = 10240
F = 384
F0 = 12
NFFT = 6000
MAXLAG = 1500
SB = 4
SRC = 8
LAGS = 3001
BLOCKS = 64
WIDE = 160
WINS = 64
LINES = 80
SLOTS = 128
ROWS = 2 * SLOTS
BINS_A = 256
BINS_B = 128
CAP = 120
PACK = 8
GRANT = 56 << 20
LAG_GRANT = 44 << 20
STEP_A = 16
STEP_B = 16
TALL = 32
LAG_TILE = 1024


def iota(shape, dim):
    return lax.broadcasted_iota(jnp.int32, shape, dim)


def one_hot(where):
    return jnp.where(where, 1.0, 0.0).astype(jnp.bfloat16)


def dot(a, b):
    return jnp.dot(a, b, preferred_element_type=jnp.float32)


def source_kernel(tm_ref, mask_ref, a0, a1, a2, b0, b1, b2, out, flag_out):
    middle = LINES // 2
    shift = SB * (1 - tm_ref[0])
    ones = lambda at: jnp.broadcast_to(mask_ref[at : at + 1, :], (16, 128)).astype(jnp.float32).astype(jnp.bfloat16)
    flags_a, flags_b = ones(0), ones(middle)
    lane = iota((128, 128), 1)
    row = iota((128, 128), 0)
    source = (lane + shift) % SRC
    here = (row == source % SB) & (lane < SRC)
    flag_out[...] = (dot(flags_a, one_hot(here & (source < SB))) + dot(flags_b, one_hot(here & (source >= SB))))[:8]
    twice = one_hot(row == lane // 2)
    kept_a, kept_b = dot(flags_a, twice), dot(flags_b, twice)
    take = iota((2 * SRC, 16), 0)
    lane = iota((2 * SRC, 16), 1)
    source = (take % SRC + shift) % SRC
    hit = lane == 2 * (source % SB) + take // SRC
    pick_a = one_hot(hit & (source < SB) & (kept_a[:, :16] > 0.5))
    pick_b = one_hot(hit & (source >= SB) & (kept_b[:, :16] > 0.5))
    rows = [
        dot(pick_a, ra.reshape(16, 128)[...]) + dot(pick_b, rb.reshape(16, 128)[...])
        for ra, rb in ((a0, b0), (a1, b1), (a2, b2))
    ]
    squares = sum(r * r for r in rows)
    energy = jnp.sum(squares[:SRC] + squares[SRC:], axis=1, keepdims=True) / F
    factor = lax.rsqrt(energy + 1e-06)
    factor = jnp.concatenate([factor, factor], axis=0)
    for k, r in enumerate(rows):
        out[0, :, k * 128 : (k + 1) * 128] = (r * factor).astype(jnp.bfloat16)


def pack_kernel(tm_ref, mask_ref, *refs):
    heads, (x0, x1, x2, send_a, send_b, slot_ref, key_ref, src_ref, flag_ref, note_ref) = refs[:6], refs[6:]
    step = pl.program_id(0)

    @pl.when(step == 0)
    def _():
        source_kernel(tm_ref, mask_ref, *heads, src_ref, flag_ref)
        flag_line = flag_ref[:1, :]
        flag_line = jnp.concatenate([flag_line, flag_line], axis=1)
        note_ref[...] = jnp.where(iota((8, BINS_A), 0) == 1, flag_line, 0.0)
        late = src_ref[0, :SRC, BINS_A:].astype(jnp.float32)
        note_ref[2:6, :BINS_B] = late[:SB]
        note_ref[2:6, BINS_B:] = late[SB:]
        lines = [mask_ref[pl.ds(k, LINES // 5, stride=5), :] for k in range(5)]
        lines = jnp.concatenate(lines, axis=1).astype(jnp.float32)
        lane = iota((WIDE, 2 * WIDE), 1)
        row = iota((WIDE, 2 * WIDE), 0)
        ahead_two, here_two = one_hot(row < lane // 2), one_hot(row == lane // 2)
        part = (iota((LINES // 5, 2 * WIDE), 1) % 2).astype(jnp.float32)
        lane = iota((WIDE, BINS_A), 1)
        row = iota((WIDE, BINS_A), 0)
        ahead, here = one_hot(row < lane), one_hot(row == lane)
        for m in range(4):
            flags = lines[:, m * WIDE : (m + 1) * WIDE].astype(jnp.bfloat16)
            slot_ref[m] = jnp.where(dot(flags, here_two) > 0.5, dot(flags, ahead_two) + part * CAP, -1.0)
            key_ref[m] = jnp.where(dot(flags, here) > 0.5, dot(flags, ahead), -1.0)

    place = iota((2 * CAP, 2 * WIDE), 0).astype(jnp.float32).astype(jnp.bfloat16)
    for n in range(PACK):
        four = pl.ds(step * (PACK // 4) + n // 4, 1)
        slot = slot_ref[n % 4, four, :].astype(jnp.bfloat16)
        pick = jnp.where(place == slot, jnp.ones_like(place), jnp.zeros_like(place))
        at = pl.ds(n * 2 * WIDE, 2 * WIDE)
        band = jnp.concatenate([r.reshape(PACK * 2 * WIDE, 128)[at, :] for r in (x0, x1, x2)], axis=1)
        rows = dot(pick, band)
        real, imag = rows[:CAP], rows[CAP:]
        energy = jnp.sum(real * real + imag * imag, axis=1, keepdims=True) / F
        factor = lax.rsqrt(energy + 1e-06)
        real = (real * factor).astype(jnp.bfloat16)
        imag = (imag * factor).astype(jnp.bfloat16)
        send_a[n, :CAP] = real[:, :BINS_A]
        send_a[n, CAP:SLOTS] = src_ref[0, :SRC, :BINS_A]
        send_a[n, SLOTS : SLOTS + CAP] = imag[:, :BINS_A]
        send_a[n, SLOTS + CAP : ROWS] = src_ref[0, SRC:, :BINS_A]
        notes = jnp.where(iota((8, BINS_A), 0) == 0, key_ref[n % 4, four, :], note_ref[...])
        send_a[n, ROWS:] = notes.astype(jnp.bfloat16)
        send_b[n, :CAP] = real[:, BINS_A:]
        send_b[n, CAP:SLOTS] = src_ref[0, SRC:, BINS_A:]
        send_b[n, SLOTS:] = imag[:, BINS_A:]


def pack(tm_index, mask, spectra):
    head = lambda k, at: pl.BlockSpec((8, 2, 128), lambda b: (at, 0, k))
    middle = BLOCKS // 2 * WIDE // 8
    band = lambda k: pl.BlockSpec((PACK * WIDE, 2, 128), lambda b: (b, 0, k))
    return pl.pallas_call(
        pack_kernel,
        grid=(BLOCKS // PACK,),
        in_specs=[
            pl.BlockSpec(memory_space=pltpu.SMEM),
            pl.BlockSpec((LINES, 128), lambda b: (0, 0)),
            *[head(k, 0) for k in range(3)],
            *[head(k, middle) for k in range(3)],
            *[band(k) for k in range(3)],
        ],
        out_specs=[
            pl.BlockSpec((PACK, ROWS + 8, BINS_A), lambda b: (b, 0, 0)),
            pl.BlockSpec((PACK, SLOTS + CAP, BINS_B), lambda b: (b, 0, 0)),
        ],
        out_shape=[
            jax.ShapeDtypeStruct((BLOCKS, ROWS + 8, BINS_A), jnp.bfloat16),
            jax.ShapeDtypeStruct((BLOCKS, SLOTS + CAP, BINS_B), jnp.bfloat16),
        ],
        scratch_shapes=[
            pltpu.VMEM((4, BLOCKS // 4, 2 * WIDE), jnp.float32),
            pltpu.VMEM((4, BLOCKS // 4, BINS_A), jnp.float32),
            pltpu.VMEM((1, 2 * SRC, F), jnp.bfloat16),
            pltpu.VMEM((8, 128), jnp.float32),
            pltpu.VMEM((8, BINS_A), jnp.float32),
        ],
        cost_estimate=pl.CostEstimate(flops=2 * BLOCKS * ROWS * 2 * WIDE * F, bytes_accessed=30_000_000, transcendentals=0),
        compiler_params=pltpu.CompilerParams(vmem_limit_bytes=GRANT),
        name="whiten_pack",
    )(tm_index, mask, *[spectra] * 9)


def spread_slots(real, imag, src_real, src_imag, pick, held, src, win, bins):
    held[win] = dot(pick, jnp.concatenate([real, imag], axis=1))
    real = src_real.astype(jnp.float32)
    imag = src_imag.astype(jnp.float32)
    for k, rows in enumerate((real, imag, real + imag)):
        for t in range(bins // 128):
            src[win, t, k * SRC : (k + 1) * SRC] = rows[:, t * 128 : (t + 1) * 128]


def correlate(held, src, total, sources, bins, steps):
    def group(i, _):
        rows = [pl.ds(pl.multiple_of(i * TALL + r, 8), 8) for r in range(0, TALL, 8)]
        for t in range(0, bins, 128):
            lanes = [slice(k * bins + t, k * bins + t + 128) for k in range(3)]
            for some in range(0, len(sources), SB):
                sums = [[[total[some + n, row, at] for row in rows] for at in lanes] for n in range(SB)]
                for win in range(steps):
                    real = [held[win, row, lanes[0]] for row in rows]
                    imag = [held[win, row, lanes[1]] for row in rows]
                    less = [x - y for x, y in zip(real, imag)]
                    for n in range(SB):
                        for k, values in enumerate((real, imag, less)):
                            a = src[win, t // 128, pl.ds(k * SRC + sources[some + n], 8, stride=0), :]
                            for r, b in enumerate(values):
                                sums[n][k][r] += a * b
                for n in range(SB):
                    for k, at in enumerate(lanes):
                        for r, row in enumerate(rows):
                            total[some + n, row, at] = sums[n][k][r]
        return 0

    lax.fori_loop(0, WIDE // TALL, group, 0)


def store_sums(total, n, out, q, bins):
    p, m, r = (total[n, :, k * bins : (k + 1) * bins] for k in range(3))
    out[q, :, :bins] = (p + m).astype(out.dtype)
    out[q, :, bins:] = (r - p + m).astype(out.dtype)


def first_kernel(got, theirs, mine, picks, count, late, held, src, total):
    step = pl.program_id(0)

    @pl.when(step == 0)
    def _():
        total[...] = jnp.zeros_like(total)
        count[...] = jnp.zeros_like(count)

    for win in range(STEP_A):
        notes = got[win, ROWS:, :].astype(jnp.float32)
        key = jnp.transpose(notes)[:WIDE, 0:1]
        pick = one_hot(iota((WIDE, SLOTS), 1) == key.astype(jnp.int32))
        picks[win] = pick
        count[...] += jnp.where(key > -0.5, 1.0, 0.0) * notes[1:2, :128]
        late[win, :SB] = notes[2:6, :BINS_B]
        late[win, SB:] = notes[2:6, BINS_B:]
        src_real, src_imag = got[win, CAP:SLOTS, :], got[win, SLOTS + CAP : ROWS, :]
        spread_slots(got[win, :SLOTS, :], got[win, SLOTS:ROWS, :], src_real, src_imag, pick, held, src, win, BINS_A)
    correlate(held, src, total, range(SRC), BINS_A, STEP_A)

    @pl.when(step == pl.num_programs(0) - 1)
    def _():
        for q in range(SB):
            store_sums(total, q, theirs, q, BINS_A)
            store_sums(total, SB + q, mine, q, BINS_A)


def first_sums(got):
    shape = (SB, WIDE, 2 * BINS_A)
    sums_spec = pl.BlockSpec(shape, lambda g: (0, 0, 0))
    return pl.pallas_call(
        first_kernel,
        grid=(WINS // STEP_A,),
        in_specs=[pl.BlockSpec((STEP_A, ROWS + 8, BINS_A), lambda g: (g, 0, 0))],
        out_specs=[
            sums_spec,
            sums_spec,
            pl.BlockSpec((STEP_A, WIDE, SLOTS), lambda g: (g, 0, 0)),
            pl.BlockSpec((WIDE, 128), lambda g: (0, 0)),
            pl.BlockSpec((STEP_A, SRC, BINS_B), lambda g: (g, 0, 0)),
        ],
        out_shape=[
            jax.ShapeDtypeStruct(shape, jnp.bfloat16),
            jax.ShapeDtypeStruct(shape, jnp.float32),
            jax.ShapeDtypeStruct((WINS, WIDE, SLOTS), jnp.bfloat16),
            jax.ShapeDtypeStruct((WIDE, 128), jnp.float32),
            jax.ShapeDtypeStruct((WINS, SRC, BINS_B), jnp.float32),
        ],
        scratch_shapes=[
            pltpu.VMEM((STEP_A, WIDE, 2 * BINS_A), jnp.float32),
            pltpu.VMEM((STEP_A, BINS_A // 128, 3 * SRC, 128), jnp.float32),
            pltpu.VMEM((SRC, WIDE, 3 * BINS_A), jnp.float32),
        ],
        cost_estimate=pl.CostEstimate(flops=30_000_000_000, bytes_accessed=20_000_000, transcendentals=0),
        compiler_params=pltpu.CompilerParams(vmem_limit_bytes=GRANT),
        name="cross_sums_first",
    )(got)


def second_kernel(first, got, late, picks, out, held, src, total):
    step = pl.program_id(0)

    @pl.when(step == 0)
    def _():
        total[...] = jnp.zeros_like(total)

    for win in range(STEP_B):
        pick = picks[win, :, :CAP]
        spread_slots(got[win, :CAP, :], got[win, SLOTS:, :], late[win], got[win, CAP:SLOTS, :], pick, held, src, win, BINS_B)
    correlate(held, src, total, range(first, first + SB), BINS_B, STEP_B)

    @pl.when(step == pl.num_programs(0) - 1)
    def _():
        for q in range(SB):
            store_sums(total, q, out, q, BINS_B)


def second_sums(got, late, picks, first, dtype, grant):
    shape = (SB, WIDE, 2 * BINS_B)
    return pl.pallas_call(
        functools.partial(second_kernel, first),
        grid=(WINS // STEP_B,),
        in_specs=[
            pl.BlockSpec((STEP_B, SLOTS + CAP, BINS_B), lambda g: (g, 0, 0)),
            pl.BlockSpec((STEP_B, SRC, BINS_B), lambda g: (g, 0, 0)),
            pl.BlockSpec((STEP_B, WIDE, SLOTS), lambda g: (g, 0, 0)),
        ],
        out_specs=pl.BlockSpec(shape, lambda g: (0, 0, 0)),
        out_shape=jax.ShapeDtypeStruct(shape, dtype),
        scratch_shapes=[
            pltpu.VMEM((STEP_B, WIDE, 2 * BINS_B), jnp.float32),
            pltpu.VMEM((STEP_B, BINS_B // 128, 3 * SRC, 128), jnp.float32),
            pltpu.VMEM((SB, WIDE, 3 * BINS_B), jnp.float32),
        ],
        cost_estimate=pl.CostEstimate(flops=8_000_000_000, bytes_accessed=8_000_000, transcendentals=0),
        compiler_params=pltpu.CompilerParams(vmem_limit_bytes=grant),
        name="cross_sums_second",
    )(got, late, picks)


def lags_kernel(mine_a, from_a, mine_b, from_b, table, count, count_from, out, held, scale):
    @pl.when(pl.program_id(0) == 0)
    def _():
        for mine, got, at in ((mine_a, from_a, slice(0, 2 * BINS_A)), (mine_b, from_b, slice(2 * BINS_A, 2 * F))):
            held[:, at] = (mine[...] + got[...].astype(jnp.float32)).astype(jnp.bfloat16)
        for q in range(SB):
            pairs = count[:, SB + q : SB + q + 1] + count_from[:, q : q + 1]
            scale[q * WIDE : (q + 1) * WIDE] = jnp.broadcast_to(1.0 / jnp.maximum(pairs, 1.0), (WIDE, 128))

    out[...] = dot(held[...], table[...]) * scale[:, 0:1]


def to_lags(mine_a, from_a, mine_b, from_b, table, count, count_from):
    rows = SB * WIDE
    full = lambda shape: pl.BlockSpec(shape, lambda n: (0, 0))
    sums = [full((rows, 2 * bins)) for bins in (BINS_A, BINS_A, BINS_B, BINS_B)]
    tiled = pl.BlockSpec((2 * F, LAG_TILE), lambda n: (0, n))
    return pl.pallas_call(
        lags_kernel,
        grid=(pl.cdiv(LAGS, LAG_TILE),),
        in_specs=[*sums, tiled, full((WIDE, 128)), full((WIDE, 128))],
        out_specs=pl.BlockSpec((rows, LAG_TILE), lambda n: (0, n)),
        out_shape=jax.ShapeDtypeStruct((rows, LAGS), jnp.float32),
        scratch_shapes=[
            pltpu.VMEM((rows, 2 * F), jnp.bfloat16),
            pltpu.VMEM((rows, 128), jnp.float32),
        ],
        cost_estimate=pl.CostEstimate(flops=4 * rows * F * LAGS, bytes_accessed=4 * rows * LAGS * 2, transcendentals=0),
        compiler_params=pltpu.CompilerParams(vmem_limit_bytes=LAG_GRANT),
        name="to_lags",
    )(*(x.reshape(rows, -1) for x in (mine_a, from_a, mine_b, from_b)), table, count, count_from)


def lag_table(zero):
    row = jnp.arange(2 * F, dtype=jnp.int32) + zero
    last = row >= 2 * BINS_A
    bins = jnp.where(last, BINS_B, BINS_A)
    inside = jnp.where(last, row - 2 * BINS_A, row)
    bin_index = F0 + jnp.where(last, BINS_A, 0) + inside % bins
    lag_index = jnp.arange(LAGS, dtype=jnp.int32) - MAXLAG
    phase_steps = jnp.mod(bin_index[:, None] * lag_index[None, :], NFFT)
    angles = phase_steps.astype(jnp.float32) * jnp.float32(2.0 * math.pi / NFFT)
    table = jnp.where((inside < bins)[:, None], jnp.cos(angles), -jnp.sin(angles))
    return table.astype(jnp.bfloat16)


def swap(x):
    return lax.ppermute(x, "tm", [(0, 1), (1, 0)])


def local(spectra, mask):
    tm_index = lax.axis_index("tm").astype(jnp.int32)[None]
    mask = mask.reshape(LINES, 128)
    spectra = spectra.reshape(CH, 2, F)
    send_a, send_b = pack(tm_index, mask, spectra)
    send_a, zero = lax.optimization_barrier((send_a, jnp.int32(0)))
    table = lag_table(zero)
    send_b, table = lax.optimization_barrier((send_b, table))
    exchange = lambda x: lax.all_to_all(x, "chan", split_axis=0, concat_axis=0, tiled=True)
    got_a = exchange(send_a)
    got_b = exchange(send_b)
    theirs_a, mine_a, picks, count, late = first_sums(got_a)
    from_a = swap(theirs_a)
    count_from = swap(count)
    got_b, count_from = lax.optimization_barrier((got_b, count_from))
    theirs_b = second_sums(got_b, late, picks, 0, jnp.bfloat16, GRANT)
    from_b = swap(theirs_b)
    mine_b = second_sums(got_b, late, picks, SB, jnp.float32, GRANT // 2)
    lagged = to_lags(mine_a, from_a, mine_b, from_b, table, count, count_from)
    return lagged.reshape(SB, WIDE, LAGS)


def solution(mesh):
    placed = (P("tm", "chan", None, None, None), P("tm", "chan", None))
    return jax.shard_map(
        local, mesh=mesh, in_specs=placed, out_specs=P("tm", "chan", None), check_vma=False
    )
```
